512 devices in a mesh: row: 32 (over x, y), col: 16 (over z, core).
Axes of the slice: x: 4, y: 8, z: 8, core: 2. Of those that a mesh axis runs over, the one named last changes fastest.
Arguments:
- window: float32 [32, 2048, 16, 256], P('row', None, 'col'), may hold values from -7 to 8, as said below
Outputs:
- factored: float32 [32, 2048, 16, 256], P('row', None, 'col')
The draws below stay inside these ranges and needn't reach their ends.
Inputs may be any that keep to these rules, and one draw needn't show every extreme that they name: `window`: entries above the diagonal are never read. The leading 2 * 128 by 256 block (lower triangle mirrored) is positive definite, with smallest eigenvalue 1 or more.
All inputs are finite; a program needn't handle non-finite values.
Results may differ from the reference program's by a relative error of at most 0.00028.
Values sent between devices are 32-bit elements; how exact they have to be, the bound alone decides.
A program may use at most 64 MiB of HBM per device.

```python
import jax
import jax.numpy as jnp
from jax import lax

ORDER = 65536
NB = 128
WCOLS = 4096
N_ROW = 32
N_COL = 16


def draw_window(key, part):
    key_diag, key_place, key_values = jax.random.split(key, 3)
    shape = (ORDER, WCOLS)
    leading = 2 * NB
    row_ids = jnp.arange(ORDER)[:, None]
    col_ids = jnp.arange(WCOLS)[None, :]
    places = jax.random.uniform(key_place, (leading,), jnp.float32, 0.0, 1.0) * leading
    diag_add = jax.random.uniform(key_diag, (leading,), jnp.float32, 1.0, 2.0)
    row_place = places[jnp.minimum(jnp.arange(ORDER), leading - 1)][:, None]
    col_place = places[jnp.minimum(jnp.arange(WCOLS), leading - 1)][None, :]
    row_add = diag_add[jnp.minimum(jnp.arange(ORDER), leading - 1)][:, None]
    kernel = jnp.exp(-jnp.abs(row_place - col_place) / 3.0)
    inner = kernel + jnp.where(row_ids == col_ids, row_add, 0.0)
    values = jax.random.truncated_normal(key_values, -3.4, 3.4, shape, jnp.float32)
    outside = jnp.where(col_ids < leading, 0.5, 1.0) * values
    matrix = jnp.where((row_ids < leading) & (col_ids < leading), inner, outside)
    return matrix.reshape(ORDER // N_ROW, N_ROW, WCOLS // N_COL, N_COL).transpose(1, 0, 3, 2)


def setup_inputs(seed: int = 0) -> dict:
    arg_keys = jax.random.split(jax.random.key(seed), 2)
    return {
        "window": draw_window(jax.random.fold_in(arg_keys[1], 71), 0),
    }


def unpack(window):
    return window.transpose(1, 0, 3, 2).reshape(ORDER, WCOLS)

def pack(matrix):
    return matrix.reshape(ORDER // N_ROW, N_ROW, WCOLS // N_COL, N_COL).transpose(1, 0, 3, 2)

def reference(window):
    matrix = unpack(window)
    for panel_step in range(2):
        start = panel_step * NB
        finish = start + NB
        diag_tile = matrix[start:finish, start:finish]
        symmetric = jnp.tril(diag_tile) + jnp.tril(diag_tile, -1).T
        factor = jnp.tril(jnp.linalg.cholesky(symmetric))
        below = matrix[finish:, start:finish]
        solved = jax.scipy.linalg.solve_triangular(factor, below.T, lower=True).T
        panel = jnp.concatenate([jnp.zeros((start, NB), jnp.float32), factor, solved], 0)
        matrix = matrix.at[:, start:finish].set(panel)
        update = jnp.dot(panel, panel[finish:WCOLS].T, precision=lax.Precision.HIGHEST)
        matrix = matrix.at[:, finish:].add(-update)
    row_ids = jnp.arange(ORDER)[:, None]
    col_ids = jnp.arange(WCOLS)[None, :]
    matrix = jnp.where(row_ids >= col_ids, matrix, 0.0)
    return pack(matrix)
```

```python
import jax
import jax.numpy as jnp
from jax import lax
from jax.experimental import pallas as pl
from jax.experimental.pallas import tpu as pltpu
from jax.sharding import PartitionSpec as P

MESH = pl.DeviceIdType.MESH
NROW = 32
NCOL = 16
ROWS = 2048
COLS = 256
HEAD = 128
HALF = ((128, 1024), (1152, 896))
HIGH = lax.Precision.HIGHEST


def gather_kernel(
    x_ref, g_ref, a_ref, b_ref,
    xv, gt, g8, abuf, bbuf,
    xsem, osem, c0s, c0r, rs, rr, bs, br, as_, ar, ks, kr,
):
    p = lax.axis_index("row")
    q = lax.axis_index("col")
    z = q // 2
    core = q % 2

    barrier = pltpu.get_barrier_semaphore()

    @pl.loop(1, NCOL)
    def _(d):
        pl.semaphore_signal(barrier, inc=1, device_id=(p, (q + d) % NCOL), device_id_type=MESH)

    @pl.loop(1, NROW)
    def _(d):
        pl.semaphore_signal(barrier, inc=1, device_id=((p + d) % NROW, q), device_id_type=MESH)

    head_in = pltpu.make_async_copy(x_ref.at[pl.ds(0, 256)], xv.at[pl.ds(0, 256)], xsem.at[0])
    rest_in = pltpu.make_async_copy(x_ref.at[pl.ds(256, 3840)], xv.at[pl.ds(256, 3840)], xsem.at[1])
    head_in.start()
    rest_in.start()
    own = pl.ds(pl.multiple_of(q * 16, 16), 16)

    head_in.wait()
    gt[own, 0:HEAD] = xv[pl.ds(0, HEAD, stride=2), :].T[0:16, :]
    pl.semaphore_wait(barrier, NCOL - 1 + NROW - 1)

    def head_copy(d):
        origin = (q + NCOL - d) % NCOL
        rows = pl.ds(pl.multiple_of(origin * 16, 16), 16)
        return own, rows

    def head_send(d):
        block = gt.at[own, pl.ds(0, HEAD)]
        return pltpu.make_async_remote_copy(
            src_ref=block, dst_ref=block, send_sem=c0s.at[d], recv_sem=c0r.at[d],
            device_id=(p, (q + d) % NCOL), device_id_type=MESH)

    def head_recv(d):
        rows = pl.ds(pl.multiple_of(((q + NCOL - d) % NCOL) * 16, 16), 16)
        block = gt.at[rows, pl.ds(0, HEAD)]
        return pltpu.make_async_remote_copy(
            src_ref=block, dst_ref=block, send_sem=c0s.at[d], recv_sem=c0r.at[d],
            device_id=(p, (q + d) % NCOL), device_id_type=MESH)

    @pl.loop(1, NCOL)
    def _(d):
        head_send(d).start()

    rest_in.wait()

    @pl.loop(1, 16)
    def _(b):
        lanes = pl.ds(pl.multiple_of(b * 128, 128), 128)
        gt[own, lanes] = xv[pl.ds(b * 256, 128, stride=2), :].T[0:16, :]

    def piece(dist, half, which):
        rows = ((z + 8 - dist) % 8) * 2 + which
        start, size = HALF[half]
        return gt.at[pl.ds(pl.multiple_of(rows * 16, 16), 16), pl.ds(start, size)]

    def ring_send(direction, step, half):
        dist = step - 1 if direction == 0 else (9 - step) % 8
        slot = step if direction == 0 else 8 - step
        to = (z + 1) % 8 if direction == 0 else (z + 7) % 8
        block = piece(dist, half, core)
        return pltpu.make_async_remote_copy(
            src_ref=block, dst_ref=block, send_sem=rs.at[direction, half, step],
            recv_sem=rr.at[half, slot], device_id=(p, to * 2 + core), device_id_type=MESH)

    def ring_recv(direction, step, half):
        slot = step if direction == 0 else 8 - step
        block = piece(slot, half, core)
        return pltpu.make_async_remote_copy(
            src_ref=block, dst_ref=block, send_sem=rs.at[direction, half, step],
            recv_sem=rr.at[half, slot], device_id=(p, q), device_id_type=MESH)

    def twin_send(slot, half):
        block = piece(slot, half, core)
        return pltpu.make_async_remote_copy(
            src_ref=block, dst_ref=block, send_sem=bs.at[half, slot],
            recv_sem=br.at[half, slot], device_id=(p, z * 2 + 1 - core), device_id_type=MESH)

    def twin_recv(slot, half):
        block = piece(slot, half, 1 - core)
        return pltpu.make_async_remote_copy(
            src_ref=block, dst_ref=block, send_sem=bs.at[half, slot],
            recv_sem=br.at[half, slot], device_id=(p, z * 2 + 1 - core), device_id_type=MESH)

    reach = {(0, 0): 4, (1, 0): 3, (0, 1): 3, (1, 1): 4}
    for half in range(2):
        ring_send(0, 1, half).start()
        ring_send(1, 1, half).start()
    for half in range(2):
        twin_send(0, half).start()

    @pl.loop(1, NCOL)
    def _(d):
        head_recv(d).wait_recv()

    g8[...] = gt[:, 0:HEAD].T[0:8, :]
    mine = pl.ds(pl.multiple_of(p * 8, 8), 8)
    abuf[mine, :] = g8[...]

    def a_send(d):
        return pltpu.make_async_remote_copy(
            src_ref=g8, dst_ref=abuf.at[mine, :], send_sem=as_.at[d], recv_sem=ar.at[d],
            device_id=((p + d) % NROW, q), device_id_type=MESH)

    def a_recv(d):
        rows = pl.ds(pl.multiple_of(((p + NROW - d) % NROW) * 8, 8), 8)
        return pltpu.make_async_remote_copy(
            src_ref=g8, dst_ref=abuf.at[rows, :], send_sem=as_.at[d], recv_sem=ar.at[d],
            device_id=((p + d) % NROW, q), device_id_type=MESH)

    @pl.loop(1, NROW)
    def _(d):
        a_send(d).start()

    def b_send(d, h):
        return pltpu.make_async_remote_copy(
            src_ref=gt.at[:, pl.ds(0, HEAD)], dst_ref=bbuf.at[h], send_sem=ks.at[d],
            recv_sem=kr.at[h], device_id=((p + d) % NROW, q), device_id_type=MESH)

    for h in range(2):
        @pl.when(p == q + 16 * h)
        def _():
            @pl.loop(1, NROW)
            def _(d):
                b_send(d, h).start()
            bbuf[h] = gt[:, 0:HEAD]

    for step in range(1, 5):
        for half in range(2):
            for direction in range(2):
                last = reach[direction, half]
                if step <= last:
                    ring_recv(direction, step, half).wait_recv()
                    if step < last:
                        ring_send(direction, step + 1, half).start()
                    slot = step if direction == 0 else 8 - step
                    twin_send(slot, half).start()

    @pl.loop(1, NROW)
    def _(d):
        a_recv(d).wait_recv()

    a_out = pltpu.make_async_copy(abuf, a_ref, osem.at[0])
    a_out.start()
    for h in range(2):
        @pl.when(p != q + 16 * h)
        def _():
            b_send(1, h).wait_recv()
    b_out = pltpu.make_async_copy(bbuf, b_ref, osem.at[1])
    b_out.start()
    for half in range(2):
        for slot in range(8):
            twin_recv(slot, half).wait_recv()
    g_out = pltpu.make_async_copy(gt, g_ref, osem.at[2])
    g_out.start()

    @pl.loop(1, NCOL)
    def _(d):
        head_send(d).wait_send()

    @pl.loop(1, NROW)
    def _(d):
        a_send(d).wait_send()

    for h in range(2):
        @pl.when(p == q + 16 * h)
        def _():
            @pl.loop(1, NROW)
            def _(d):
                b_send(d, h).wait_send()

    for half in range(2):
        for direction in range(2):
            for step in range(1, reach[direction, half] + 1):
                ring_send(direction, step, half).wait_send()
        for slot in range(8):
            twin_send(slot, half).wait_send()
    a_out.wait()
    b_out.wait()
    g_out.wait()


def gather(x):
    dma = pltpu.SemaphoreType.DMA
    f32 = jnp.float32
    any_spec = pl.BlockSpec(memory_space=pl.ANY)
    return pl.pallas_call(
        gather_kernel,
        out_shape=(
            jax.ShapeDtypeStruct((256, ROWS), f32),
            jax.ShapeDtypeStruct((256, 256), f32),
            jax.ShapeDtypeStruct((2, 256, HEAD), f32),
        ),
        in_specs=[any_spec],
        out_specs=(any_spec, any_spec, any_spec),
        scratch_shapes=[
            pltpu.VMEM((2 * ROWS, 128), f32),
            pltpu.VMEM((256, ROWS), f32),
            pltpu.VMEM((8, 256), f32),
            pltpu.VMEM((256, 256), f32),
            pltpu.VMEM((2, 256, HEAD), f32),
            dma((2,)), dma((3,)),
            dma((NCOL,)), dma((NCOL,)),
            dma((2, 2, 5)), dma((2, 8)),
            dma((2, 8)), dma((2, 8)),
            dma((NROW,)), dma((NROW,)),
            dma((NROW,)), dma((2,)),
        ],
        compiler_params=pltpu.CompilerParams(
            collective_id=0, has_side_effects=True, vmem_limit_bytes=24 << 20),
        name="gather",
    )(x)


def update_kernel(g_ref, w_ref, l_ref, x_ref, o_ref):
    p = lax.axis_index("row")
    q = lax.axis_index("col")
    size = g_ref.shape[1]
    first = pl.program_id(0) * size
    acc = lax.dot_general(
        g_ref[...], w_ref[...], (((0,), (0,)), ((), ())), precision=HIGH,
        preferred_element_type=jnp.float32)
    row = (first + lax.broadcasted_iota(jnp.int32, (size, 128), 0)) * NROW + p
    lane = lax.broadcasted_iota(jnp.int32, (size, 128), 1)
    left = jnp.where(lane < 16, acc[:, :128], x_ref[pl.ds(0, size, stride=2), :] - acc[:, :128])
    right = x_ref[pl.ds(1, size, stride=2), :] - acc[:, 128:]
    o_ref[pl.ds(0, size, stride=2), :] = jnp.where(row >= lane * NCOL + q, left, 0.0)
    o_ref[pl.ds(1, size, stride=2), :] = jnp.where(row >= (lane + 128) * NCOL + q, right, 0.0)

    @pl.when(pl.program_id(0) == 0)
    def _():
        keep = row[0:8] >= lane[0:8] * NCOL + q
        o_ref[pl.ds(0, 8, stride=2), :] = jnp.where(keep, l_ref[...], 0.0)


def update(g, w, l8, x):
    size = 512
    return pl.pallas_call(
        update_kernel,
        grid=(ROWS // size,),
        out_shape=jax.ShapeDtypeStruct((2 * ROWS, 128), jnp.float32),
        in_specs=[
            pl.BlockSpec((256, size), lambda i: (0, i)),
            pl.BlockSpec((256, 256), lambda i: (0, 0)),
            pl.BlockSpec((8, 128), lambda i: (0, 0)),
            pl.BlockSpec((2 * size, 128), lambda i: (i, 0)),
        ],
        out_specs=pl.BlockSpec((2 * size, 128), lambda i: (i, 0)),
        compiler_params=pltpu.CompilerParams(vmem_limit_bytes=24 << 20),
        name="update",
    )(g, w, l8, x)


def body(window):
    x = window.reshape(2 * ROWS, 128)
    p = lax.axis_index("row")
    q = lax.axis_index("col")
    g, a, b = gather(x)
    natural = a.reshape(NROW, 8, NCOL, 16).transpose(1, 0, 3, 2).reshape(256, 256)
    symmetric = jnp.tril(natural) + jnp.tril(natural, -1).T
    factor = jnp.tril(jnp.linalg.cholesky(symmetric))
    inverse = jax.scipy.linalg.solve_triangular(factor, jnp.eye(256, dtype=jnp.float32), lower=True)
    cols = b.reshape(2, NCOL, 16, HEAD).transpose(2, 1, 3, 0).reshape(256, 256)
    t = jnp.dot(inverse, cols, precision=HIGH)
    col_id = jnp.arange(256)[:, None]
    lane = jnp.arange(256)[None, :]
    pick = (col_id == lane * NCOL + q).astype(jnp.float32)
    t = jnp.where(lane < 16, pick, t)
    w = jnp.dot(inverse.T, t, precision=HIGH)
    w = w.reshape(16, NCOL, 256).transpose(1, 0, 2).reshape(256, 256)
    rows8 = lax.dynamic_index_in_dim(factor.reshape(8, NROW, 256), p, 1, False)
    l8 = lax.dynamic_index_in_dim(rows8.reshape(8, 16, NCOL), q, 2, False)
    l8 = jnp.pad(l8, ((0, 0), (0, 112)))
    out = update(g, w, l8, x)
    return out.reshape(1, ROWS, 1, COLS)


def solution(mesh):
    spec = P("row", None, "col", None)
    return jax.shard_map(body, mesh=mesh, in_specs=(spec,), out_specs=spec, check_vma=False)
```

```python
import jax
import jax.numpy as jnp
from jax import lax
from jax.experimental import pallas as pl
from jax.experimental.pallas import tpu as pltpu
from jax.sharding import PartitionSpec as P

MESH = pl.DeviceIdType.MESH
NROW = 32
NCOL = 16
ROWS = 2048
COLS = 256
HEAD = 128
HALF = ((128, 1024), (1152, 896))
HIGH = lax.Precision.HIGHEST


def gather_kernel(
    x_ref, g_ref, a_ref, b_ref,
    xv, gt, g8, b8, abuf, bbuf,
    xsem, osem, c0s, c0r, rs, rr, bs, br, as_, ar, ks, kr, ts, tr,
):
    p = lax.axis_index("row")
    q = lax.axis_index("col")
    z = q // 2
    core = q % 2

    barrier = pltpu.get_barrier_semaphore()

    @pl.loop(1, NCOL)
    def _(d):
        pl.semaphore_signal(barrier, inc=1, device_id=(p, (q + d) % NCOL), device_id_type=MESH)

    @pl.loop(1, NROW)
    def _(d):
        pl.semaphore_signal(barrier, inc=1, device_id=((p + d) % NROW, q), device_id_type=MESH)

    for half in range(2):
        @pl.when((q * 2 + half != p) | (p % NCOL != q))
        def _():
            pl.semaphore_signal(
                barrier, inc=1, device_id=(q * 2 + half, p % NCOL), device_id_type=MESH)

        @pl.when((q + 16 * half != p) | (p // 2 != q))
        def _():
            pl.semaphore_signal(
                barrier, inc=1, device_id=(q + 16 * half, p // 2), device_id_type=MESH)

    head_in = pltpu.make_async_copy(x_ref.at[pl.ds(0, 256)], xv.at[pl.ds(0, 256)], xsem.at[0])
    rest_in = pltpu.make_async_copy(x_ref.at[pl.ds(256, 3840)], xv.at[pl.ds(256, 3840)], xsem.at[1])
    head_in.start()
    rest_in.start()
    own = pl.ds(pl.multiple_of(q * 16, 16), 16)

    head_in.wait()
    gt[own, 0:HEAD] = xv[pl.ds(0, HEAD, stride=2), :].T[0:16, :]
    waits = NCOL - 1 + NROW - 1
    for half in range(2):
        waits += jnp.where((q * 2 + half != p) | (p % NCOL != q), 1, 0)
        waits += jnp.where((q + 16 * half != p) | (p // 2 != q), 1, 0)
    pl.semaphore_wait(barrier, waits)

    def head_send(d):
        block = gt.at[own, pl.ds(0, HEAD)]
        return pltpu.make_async_remote_copy(
            src_ref=block, dst_ref=block, send_sem=c0s.at[d], recv_sem=c0r.at[d],
            device_id=(p, (q + d) % NCOL), device_id_type=MESH)

    def head_recv(d):
        rows = pl.ds(pl.multiple_of(((q + NCOL - d) % NCOL) * 16, 16), 16)
        block = gt.at[rows, pl.ds(0, HEAD)]
        return pltpu.make_async_remote_copy(
            src_ref=block, dst_ref=block, send_sem=c0s.at[d], recv_sem=c0r.at[d],
            device_id=(p, (q + d) % NCOL), device_id_type=MESH)

    @pl.loop(1, NCOL)
    def _(d):
        head_send(d).start()

    side = pl.ds(pl.multiple_of((p // NCOL) * HEAD, HEAD), HEAD)

    def scatter_send(half):
        rows = pl.ds(pl.multiple_of(q * 16 + half * 8, 8), 8)
        return pltpu.make_async_remote_copy(
            src_ref=gt.at[rows, pl.ds(0, HEAD)], dst_ref=b8.at[:, side], send_sem=ts.at[half],
            recv_sem=tr.at[p // NCOL], device_id=(q * 2 + half, p % NCOL), device_id_type=MESH)

    def scatter_recv(h):
        return pltpu.make_async_remote_copy(
            src_ref=b8.at[:, pl.ds(h * HEAD, HEAD)], dst_ref=b8.at[:, pl.ds(h * HEAD, HEAD)],
            send_sem=ts.at[0], recv_sem=tr.at[h], device_id=(q * 2, p % NCOL), device_id_type=MESH)

    for half in range(2):
        @pl.when((q * 2 + half != p) | (p % NCOL != q))
        def _():
            scatter_send(half).start()

        @pl.when((q * 2 + half == p) & (p % NCOL == q))
        def _():
            rows = pl.ds(pl.multiple_of(q * 16 + half * 8, 8), 8)
            b8[:, side] = gt[rows, 0:HEAD]

    rest_in.wait()

    @pl.loop(1, 16)
    def _(b):
        lanes = pl.ds(pl.multiple_of(b * 128, 128), 128)
        gt[own, lanes] = xv[pl.ds(b * 256, 128, stride=2), :].T[0:16, :]

    def piece(dist, half, which):
        rows = ((z + 8 - dist) % 8) * 2 + which
        start, size = HALF[half]
        return gt.at[pl.ds(pl.multiple_of(rows * 16, 16), 16), pl.ds(start, size)]

    def ring_send(direction, step, half):
        dist = step - 1 if direction == 0 else (9 - step) % 8
        slot = step if direction == 0 else 8 - step
        to = (z + 1) % 8 if direction == 0 else (z + 7) % 8
        block = piece(dist, half, core)
        return pltpu.make_async_remote_copy(
            src_ref=block, dst_ref=block, send_sem=rs.at[direction, half, step],
            recv_sem=rr.at[half, slot], device_id=(p, to * 2 + core), device_id_type=MESH)

    def ring_recv(direction, step, half):
        slot = step if direction == 0 else 8 - step
        block = piece(slot, half, core)
        return pltpu.make_async_remote_copy(
            src_ref=block, dst_ref=block, send_sem=rs.at[direction, half, step],
            recv_sem=rr.at[half, slot], device_id=(p, q), device_id_type=MESH)

    def twin_send(slot, half):
        block = piece(slot, half, core)
        return pltpu.make_async_remote_copy(
            src_ref=block, dst_ref=block, send_sem=bs.at[half, slot],
            recv_sem=br.at[half, slot], device_id=(p, z * 2 + 1 - core), device_id_type=MESH)

    def twin_recv(slot, half):
        block = piece(slot, half, 1 - core)
        return pltpu.make_async_remote_copy(
            src_ref=block, dst_ref=block, send_sem=bs.at[half, slot],
            recv_sem=br.at[half, slot], device_id=(p, z * 2 + 1 - core), device_id_type=MESH)

    reach = {(0, 0): 4, (1, 0): 3, (0, 1): 3, (1, 1): 4}
    for half in range(2):
        ring_send(0, 1, half).start()
        ring_send(1, 1, half).start()
    for half in range(2):
        twin_send(0, half).start()

    @pl.loop(1, NCOL)
    def _(d):
        head_recv(d).wait_recv()

    g8[...] = gt[:, 0:HEAD].T[0:8, :]
    mine = pl.ds(pl.multiple_of(p * 8, 8), 8)
    abuf[mine, :] = g8[...]

    def a_send(d):
        return pltpu.make_async_remote_copy(
            src_ref=g8, dst_ref=abuf.at[mine, :], send_sem=as_.at[d], recv_sem=ar.at[d],
            device_id=((p + d) % NROW, q), device_id_type=MESH)

    def a_recv(d):
        rows = pl.ds(pl.multiple_of(((p + NROW - d) % NROW) * 8, 8), 8)
        return pltpu.make_async_remote_copy(
            src_ref=g8, dst_ref=abuf.at[rows, :], send_sem=as_.at[d], recv_sem=ar.at[d],
            device_id=((p + d) % NROW, q), device_id_type=MESH)

    @pl.loop(1, NROW)
    def _(d):
        a_send(d).start()

    for h in range(2):
        @pl.when((q + 16 * h != p) | (p // 2 != q))
        def _():
            scatter_recv(h).wait_recv()
    bbuf[mine, :] = b8[...]

    def b_send(d):
        return pltpu.make_async_remote_copy(
            src_ref=b8, dst_ref=bbuf.at[mine, :], send_sem=ks.at[d], recv_sem=kr.at[d],
            device_id=((p + d) % NROW, q), device_id_type=MESH)

    def b_recv(d):
        rows = pl.ds(pl.multiple_of(((p + NROW - d) % NROW) * 8, 8), 8)
        return pltpu.make_async_remote_copy(
            src_ref=b8, dst_ref=bbuf.at[rows, :], send_sem=ks.at[d], recv_sem=kr.at[d],
            device_id=((p + d) % NROW, q), device_id_type=MESH)

    @pl.loop(1, NROW)
    def _(d):
        b_send(d).start()

    for step in range(1, 5):
        for half in range(2):
            for direction in range(2):
                last = reach[direction, half]
                if step <= last:
                    ring_recv(direction, step, half).wait_recv()
                    if step < last:
                        ring_send(direction, step + 1, half).start()
                    slot = step if direction == 0 else 8 - step
                    twin_send(slot, half).start()

    @pl.loop(1, NROW)
    def _(d):
        a_recv(d).wait_recv()

    a_out = pltpu.make_async_copy(abuf, a_ref, osem.at[0])
    a_out.start()

    @pl.loop(1, NROW)
    def _(d):
        b_recv(d).wait_recv()

    b_out = pltpu.make_async_copy(bbuf, b_ref, osem.at[1])
    b_out.start()
    for half in range(2):
        for slot in range(8):
            twin_recv(slot, half).wait_recv()
    g_out = pltpu.make_async_copy(gt, g_ref, osem.at[2])
    g_out.start()

    @pl.loop(1, NCOL)
    def _(d):
        head_send(d).wait_send()

    @pl.loop(1, NROW)
    def _(d):
        a_send(d).wait_send()

    @pl.loop(1, NROW)
    def _(d):
        b_send(d).wait_send()

    for half in range(2):
        @pl.when((q * 2 + half != p) | (p % NCOL != q))
        def _():
            scatter_send(half).wait_send()

    for half in range(2):
        for direction in range(2):
            for step in range(1, reach[direction, half] + 1):
                ring_send(direction, step, half).wait_send()
        for slot in range(8):
            twin_send(slot, half).wait_send()
    a_out.wait()
    b_out.wait()
    g_out.wait()


def gather(x):
    dma = pltpu.SemaphoreType.DMA
    f32 = jnp.float32
    any_spec = pl.BlockSpec(memory_space=pltpu.HBM)
    return pl.pallas_call(
        gather_kernel,
        out_shape=(
            jax.ShapeDtypeStruct((256, ROWS), f32),
            jax.ShapeDtypeStruct((256, 256), f32),
            jax.ShapeDtypeStruct((256, 256), f32),
        ),
        in_specs=[any_spec],
        out_specs=(any_spec, any_spec, any_spec),
        scratch_shapes=[
            pltpu.VMEM((2 * ROWS, 128), f32),
            pltpu.VMEM((256, ROWS), f32),
            pltpu.VMEM((8, 256), f32),
            pltpu.VMEM((8, 256), f32),
            pltpu.VMEM((256, 256), f32),
            pltpu.VMEM((256, 256), f32),
            dma((2,)), dma((3,)),
            dma((NCOL,)), dma((NCOL,)),
            dma((2, 2, 5)), dma((2, 8)),
            dma((2, 8)), dma((2, 8)),
            dma((NROW,)), dma((NROW,)),
            dma((NROW,)), dma((NROW,)),
            dma((2,)), dma((2,)),
        ],
        compiler_params=pltpu.CompilerParams(
            collective_id=0, has_side_effects=True, vmem_limit_bytes=24 << 20),
        name="gather",
    )(x)


def mm(a, b, ca=1, cb=0):
    return lax.dot_general(a, b, (((ca,), (cb,)), ((), ())), precision=HIGH, preferred_element_type=jnp.float32)

def lane_bcast(v, c):
    return jnp.broadcast_to(v[:, c:c+1], (8, 128))

def sub_bcast(v, r):
    return jnp.broadcast_to(v[r:r+1, :], (8, 128))

def invert_factor(m):
    lane = lax.broadcasted_iota(jnp.int32, (8, 128), 1)
    sub = lax.broadcasted_iota(jnp.int32, (8, 128), 0)
    m = list(m)
    out = []
    for j in range(16):
        inside = (lane >= 8*j) & (lane < 8*j+8)
        own = [lane_bcast(m[j], 8*j+k) for k in range(8)]
        e = {(i, k): sub_bcast(own[k], i) for k in range(8) for i in range(k, 8)}
        r = []
        for k in range(8):
            rk = lax.rsqrt(e[k, k])
            r.append(rk)
            for i in range(k+1, 8):
                e[i, k] = e[i, k] * rk
            for c in range(k+1, 8):
                for i in range(c, 8):
                    e[i, c] = e[i, c] - e[i, k] * e[c, k]
        row = jnp.where(inside, jnp.where(lane == sub + 8*j, 1.0, 0.0), m[j])
        final = jnp.zeros((8, 128), jnp.float32)
        ups = []
        for k in range(8):
            u = sub_bcast(row, k) * r[k]
            ups.append(u)
            final = jnp.where(sub == k, u, final)
            if k < 7:
                l = own[k] * r[k]
                row = row - l * u
                for c in range(k+1, 8):
                    own[c] = own[c] - l * e[c, k]
        out.append(jnp.where(lane < 8*j+8, final, 0.0))
        for i in range(j+1, 16):
            d = [lane_bcast(m[i], 8*j+k) for k in range(8)]
            acc = jnp.where(inside, 0.0, m[i])
            for k in range(8):
                l = d[k] * r[k]
                acc = acc - l * ups[k]
                for c in range(k+1, 8):
                    d[c] = d[c] - l * e[c, k]
            m[i] = acc
    return out


def one_hot(match):
    return jnp.where(match, 1.0, 0.0)


def factor_kernel(a_ref, b_ref, w_ref, h_ref, sym, z_ref):
    p = lax.axis_index("row")
    q = lax.axis_index("col")
    row = lax.broadcasted_iota(jnp.int32, (256, 256), 0)
    col = lax.broadcasted_iota(jnp.int32, (256, 256), 1)
    row_order = one_hot(row == (col % 8) * NROW + col // 8)
    col_order = one_hot(col == (row % 16) * NCOL + row // 16)
    rows = mm(row_order, a_ref[...])
    sym[...] = jnp.where(row >= col, mm(rows, col_order), mm(col_order, rows, 0, 1))
    pick = one_hot(row[0:8] * NROW + p == col[0:8])
    h_ref[...] = mm(mm(pick, sym[...]), col_order, 1, 1)

    z1 = invert_factor([sym[8 * i:8 * i + 8, 0:128] for i in range(16)])
    for i in range(16):
        z_ref[8 * i:8 * i + 8, 0:128] = z1[i]
    z1 = z_ref[0:128, 0:128]
    low = mm(sym[128:256, 0:128], z1, 1, 1)
    schur = sym[128:256, 128:256] - mm(low, low, 1, 1)
    carry = mm(low, z1)
    z2 = invert_factor([schur[8 * i:8 * i + 8] for i in range(16)])
    for i in range(16):
        z_ref[128 + 8 * i:136 + 8 * i, 128:256] = z2[i]
    z_ref[128:256, 0:128] = -mm(z_ref[128:256, 128:256], carry)
    z_ref[0:128, 128:256] = jnp.zeros((128, 128), jnp.float32)

    z = mm(z_ref[...], col_order, 1, 1)
    mixed = mm(z, b_ref[...])
    side = one_hot(col == (row % 128) * 2 + row // 128)
    t = jnp.where(col < 16, one_hot(row == col * NCOL + q), mm(mixed, side))
    w_ref[...] = mm(z, t, 0, 0)


def factor(a, b):
    vmem = pl.BlockSpec(memory_space=pltpu.VMEM)
    return pl.pallas_call(
        factor_kernel,
        out_shape=(
            jax.ShapeDtypeStruct((256, 256), jnp.float32),
            jax.ShapeDtypeStruct((8, 256), jnp.float32),
        ),
        in_specs=[vmem, vmem],
        out_specs=(vmem, vmem),
        scratch_shapes=[pltpu.VMEM((256, 256), jnp.float32), pltpu.VMEM((256, 256), jnp.float32)],
        compiler_params=pltpu.CompilerParams(vmem_limit_bytes=24 << 20),
        name="factor",
    )(a, b)


def update_kernel(g_ref, w_ref, h_ref, x_ref, o_ref):
    p = lax.axis_index("row")
    q = lax.axis_index("col")
    size = g_ref.shape[1]
    first = pl.program_id(0) * size
    acc = lax.dot_general(
        g_ref[...], w_ref[...], (((0,), (0,)), ((), ())), precision=HIGH,
        preferred_element_type=jnp.float32)
    row = (first + lax.broadcasted_iota(jnp.int32, (size, 128), 0)) * NROW + p
    lane = lax.broadcasted_iota(jnp.int32, (size, 128), 1)
    left = jnp.where(lane < 16, acc[:, :128], x_ref[pl.ds(0, size, stride=2), :] - acc[:, :128])
    right = x_ref[pl.ds(1, size, stride=2), :] - acc[:, 128:]
    o_ref[pl.ds(0, size, stride=2), :] = jnp.where(row >= lane * NCOL + q, left, 0.0)
    o_ref[pl.ds(1, size, stride=2), :] = jnp.where(row >= (lane + 128) * NCOL + q, right, 0.0)

    @pl.when(pl.program_id(0) == 0)
    def _():
        keep = row[0:8] >= lane[0:8] * NCOL + q
        o_ref[pl.ds(0, 8, stride=2), :] = jnp.where(keep & (lane[0:8] < 16), mm(h_ref[...], w_ref[:, 0:128]), 0.0)


def update(g, w, h, x):
    size = 512
    return pl.pallas_call(
        update_kernel,
        grid=(ROWS // size,),
        out_shape=jax.ShapeDtypeStruct((2 * ROWS, 128), jnp.float32),
        in_specs=[
            pl.BlockSpec((256, size), lambda i: (0, i)),
            pl.BlockSpec((256, 256), lambda i: (0, 0)),
            pl.BlockSpec((8, 256), lambda i: (0, 0)),
            pl.BlockSpec((2 * size, 128), lambda i: (i, 0)),
        ],
        out_specs=pl.BlockSpec((2 * size, 128), lambda i: (i, 0)),
        compiler_params=pltpu.CompilerParams(vmem_limit_bytes=24 << 20),
        name="update",
    )(g, w, h, x)


def body(window):
    x = window.reshape(2 * ROWS, 128)
    g, a, b = gather(x)
    w, h = factor(a, b)
    out = update(g, w, h, x)
    return out.reshape(1, ROWS, 1, COLS)


def solution(mesh):
    spec = P("row", None, "col", None)
    return jax.shard_map(body, mesh=mesh, in_specs=(spec,), out_specs=spec, check_vma=False)
```

```python
import jax
import jax.numpy as jnp
from jax import lax
from jax.experimental import pallas as pl
from jax.experimental.pallas import tpu as pltpu
from jax.sharding import PartitionSpec as P

MESH = pl.DeviceIdType.MESH
NROW = 32
NCOL = 16
ROWS = 2048
COLS = 256
HEAD = 128
HALF = ((128, 1024), (1152, 896))
REACH = {(0, 0): 4, (1, 0): 3, (0, 1): 3, (1, 1): 4}
HIGH = lax.Precision.HIGHEST


def mm(a, b, ca=1, cb=0):
    return lax.dot_general(a, b, (((ca,), (cb,)), ((), ())), precision=HIGH, preferred_element_type=jnp.float32)

def lane_bcast(v, c):
    return jnp.broadcast_to(v[:, c:c+1], (8, 128))

def sub_bcast(v, r):
    return jnp.broadcast_to(v[r:r+1, :], (8, 128))

def invert_factor(m):
    lane = lax.broadcasted_iota(jnp.int32, (8, 128), 1)
    sub = lax.broadcasted_iota(jnp.int32, (8, 128), 0)
    m = list(m)
    out = []
    for j in range(16):
        inside = (lane >= 8*j) & (lane < 8*j+8)
        own = [lane_bcast(m[j], 8*j+k) for k in range(8)]
        e = {(i, k): sub_bcast(own[k], i) for k in range(8) for i in range(k, 8)}
        r = []
        for k in range(8):
            rk = lax.rsqrt(e[k, k])
            r.append(rk)
            for i in range(k+1, 8):
                e[i, k] = e[i, k] * rk
            for c in range(k+1, 8):
                for i in range(c, 8):
                    e[i, c] = e[i, c] - e[i, k] * e[c, k]
        row = jnp.where(inside, jnp.where(lane == sub + 8*j, 1.0, 0.0), m[j])
        final = jnp.zeros((8, 128), jnp.float32)
        ups = []
        for k in range(8):
            u = sub_bcast(row, k) * r[k]
            ups.append(u)
            final = jnp.where(sub == k, u, final)
            if k < 7:
                l = own[k] * r[k]
                row = row - l * u
                for c in range(k+1, 8):
                    own[c] = own[c] - l * e[c, k]
        out.append(jnp.where(lane < 8*j+8, final, 0.0))
        for i in range(j+1, 16):
            d = [lane_bcast(m[i], 8*j+k) for k in range(8)]
            acc = jnp.where(inside, 0.0, m[i])
            for k in range(8):
                l = d[k] * r[k]
                acc = acc - l * ups[k]
                for c in range(k+1, 8):
                    d[c] = d[c] - l * e[c, k]
            m[i] = acc
    return out


def parts(v):
    high = v.astype(jnp.bfloat16)
    rest = v - high.astype(jnp.float32)
    middle = rest.astype(jnp.bfloat16)
    return high, middle, (rest - middle.astype(jnp.float32)).astype(jnp.bfloat16)


def one_hot(match):
    return jnp.where(match, 1.0, 0.0).astype(jnp.bfloat16)


def pick_left(chosen, v, ca=1, cb=0):
    return sum(
        lax.dot_general(chosen, part, (((ca,), (cb,)), ((), ())), preferred_element_type=jnp.float32)
        for part in parts(v))


def pick_right(v, chosen, ca=1, cb=0):
    return sum(
        lax.dot_general(part, chosen, (((ca,), (cb,)), ((), ())), preferred_element_type=jnp.float32)
        for part in parts(v))


def panel_kernel(
    x_ref, g_ref, w_ref, h_ref,
    xv, own, head, g8, b8, abuf, bbuf, sym, work, carry, zd, zb,
    xsem, osem, hs, hr, rs, rr, bs, br, as_, ar, ks, kr, ts, tr, us, ur,
):
    p = lax.axis_index("row")
    q = lax.axis_index("col")
    z = q // 2
    core = q % 2
    twin = (p, z * 2 + 1 - core)
    block = core * 16 + z * 2
    feeder = 2 * ((p % NCOL) // 2) + p // NCOL

    def to_self(half):
        return (block + half == p) & (p % NCOL == q)

    def from_self(h):
        return (q + 16 * h == p) & (feeder == q)

    barrier = pltpu.get_barrier_semaphore()

    @pl.loop(1, 8)
    def _(d):
        pl.semaphore_signal(
            barrier, inc=1, device_id=(p, ((z + d) % 8) * 2 + core), device_id_type=MESH)

    pl.semaphore_signal(barrier, inc=1, device_id=twin, device_id_type=MESH)

    @pl.loop(1, NROW)
    def _(d):
        pl.semaphore_signal(barrier, inc=1, device_id=((p + d) % NROW, q), device_id_type=MESH)

    waits = 7 + 1 + NROW - 1
    for half in range(2):
        @pl.when(jnp.logical_not(to_self(half)))
        def _():
            pl.semaphore_signal(
                barrier, inc=1, device_id=(block + half, p % NCOL), device_id_type=MESH)

        @pl.when(jnp.logical_not(from_self(half)))
        def _():
            pl.semaphore_signal(
                barrier, inc=1, device_id=(q + 16 * half, feeder), device_id_type=MESH)

        waits += jnp.where(to_self(half), 0, 1) + jnp.where(from_self(half), 0, 1)

    head_in = pltpu.make_async_copy(x_ref.at[pl.ds(0, 256)], xv.at[pl.ds(0, 256)], xsem.at[0])
    rest_in = pltpu.make_async_copy(x_ref.at[pl.ds(256, 3840)], xv.at[pl.ds(256, 3840)], xsem.at[1])
    head_in.start()
    rest_in.start()
    head_in.wait()
    own[:, 0:HEAD] = xv[pl.ds(0, HEAD, stride=2), :].T[0:16, :]
    head[pl.ds(pl.multiple_of(z * 16, 16), 16), :] = own[:, 0:HEAD]
    rest_in.wait()

    @pl.loop(1, 16)
    def _(b):
        lanes = pl.ds(pl.multiple_of(b * 128, 128), 128)
        own[:, lanes] = xv[pl.ds(b * 256, 128, stride=2), :].T[0:16, :]

    pl.semaphore_wait(barrier, waits)

    def head_copy(d, origin):
        rows = pl.ds(pl.multiple_of(origin * 16, 16), 16)
        return pltpu.make_async_remote_copy(
            src_ref=own.at[:, pl.ds(0, HEAD)], dst_ref=head.at[rows, :], send_sem=hs.at[d],
            recv_sem=hr.at[d], device_id=(p, ((z + d) % 8) * 2 + core), device_id_type=MESH)

    @pl.loop(1, 8)
    def _(d):
        head_copy(d, z).start()

    side = pl.ds(pl.multiple_of((p // NCOL) * HEAD, HEAD), HEAD)

    def scatter_send(half):
        return pltpu.make_async_remote_copy(
            src_ref=own.at[pl.ds(half * 8, 8), pl.ds(0, HEAD)], dst_ref=b8.at[:, side],
            send_sem=ts.at[half], recv_sem=tr.at[p // NCOL],
            device_id=(block + half, p % NCOL), device_id_type=MESH)

    def scatter_recv(h):
        lanes = b8.at[:, pl.ds(h * HEAD, HEAD)]
        return pltpu.make_async_remote_copy(
            src_ref=lanes, dst_ref=lanes, send_sem=ts.at[0], recv_sem=tr.at[h],
            device_id=(block, p % NCOL), device_id_type=MESH)

    for half in range(2):
        @pl.when(jnp.logical_not(to_self(half)))
        def _():
            scatter_send(half).start()

        @pl.when(to_self(half))
        def _():
            b8[:, side] = own[half * 8:half * 8 + 8, 0:HEAD]

    def piece(dist, half, which):
        rows = which * 128 + ((z + 8 - dist) % 8) * 16
        start, size = HALF[half]
        return g_ref.at[pl.ds(pl.multiple_of(rows, 16), 16), pl.ds(start, size)]

    def source(dist, half):
        start, size = HALF[half]
        return own.at[:, pl.ds(start, size)] if dist == 0 else piece(dist, half, core)

    def ring_send(direction, step, half):
        dist = step - 1 if direction == 0 else (9 - step) % 8
        slot = step if direction == 0 else 8 - step
        to = (z + 1) % 8 if direction == 0 else (z + 7) % 8
        return pltpu.make_async_remote_copy(
            src_ref=source(dist, half), dst_ref=piece(dist, half, core),
            send_sem=rs.at[direction, half, step], recv_sem=rr.at[half, slot],
            device_id=(p, to * 2 + core), device_id_type=MESH)

    def ring_recv(direction, step, half):
        slot = step if direction == 0 else 8 - step
        return pltpu.make_async_remote_copy(
            src_ref=piece(slot, half, core), dst_ref=piece(slot, half, core),
            send_sem=rs.at[direction, half, step], recv_sem=rr.at[half, slot],
            device_id=twin, device_id_type=MESH)

    def twin_send(slot, half):
        return pltpu.make_async_remote_copy(
            src_ref=source(slot, half), dst_ref=piece(slot, half, core),
            send_sem=bs.at[half, slot], recv_sem=br.at[half, slot],
            device_id=twin, device_id_type=MESH)

    def twin_recv(slot, half):
        return pltpu.make_async_remote_copy(
            src_ref=piece(slot, half, 1 - core), dst_ref=piece(slot, half, 1 - core),
            send_sem=bs.at[half, slot], recv_sem=br.at[half, slot],
            device_id=twin, device_id_type=MESH)

    def ring_step(step):
        for half in range(2):
            for direction in range(2):
                last = REACH[direction, half]
                if step <= last:
                    ring_recv(direction, step, half).wait_recv()
                    if step < last:
                        ring_send(direction, step + 1, half).start()
                    twin_send(step if direction == 0 else 8 - step, half).start()

    for half in range(2):
        ring_send(0, 1, half).start()
        ring_send(1, 1, half).start()

    @pl.loop(1, 8)
    def _(d):
        head_copy(d, (z + 8 - d) % 8).wait_recv()

    g8[...] = head[...].T[0:8, :]
    mine = pl.ds(pl.multiple_of(p * 8, 8), 8)
    abuf[core, mine, :] = g8[...]

    def a_copy(d, origin):
        rows = pl.ds(pl.multiple_of(origin * 8, 8), 8)
        return pltpu.make_async_remote_copy(
            src_ref=g8, dst_ref=abuf.at[core, rows, :], send_sem=as_.at[d], recv_sem=ar.at[d],
            device_id=((p + d) % NROW, q), device_id_type=MESH)

    @pl.loop(1, NROW)
    def _(d):
        a_copy(d, p).start()

    for h in range(2):
        @pl.when(jnp.logical_not(from_self(h)))
        def _():
            scatter_recv(h).wait_recv()
    bbuf[mine, :] = b8[...]

    def b_copy(d, origin):
        rows = pl.ds(pl.multiple_of(origin * 8, 8), 8)
        return pltpu.make_async_remote_copy(
            src_ref=b8, dst_ref=bbuf.at[rows, :], send_sem=ks.at[d], recv_sem=kr.at[d],
            device_id=((p + d) % NROW, q), device_id_type=MESH)

    @pl.loop(1, NROW)
    def _(d):
        b_copy(d, p).start()

    def lead(which):
        return g_ref.at[pl.ds(pl.multiple_of(which * 128, 128), 128), pl.ds(0, HEAD)]

    lead_here = pltpu.make_async_copy(head, lead(core), osem.at[0])
    lead_here.start()
    own_rows = pl.ds(pl.multiple_of(core * 128 + z * 16, 16), 16)
    own_here = pltpu.make_async_copy(
        own.at[:, pl.ds(HEAD, ROWS - HEAD)], g_ref.at[own_rows, pl.ds(HEAD, ROWS - HEAD)],
        osem.at[1])
    own_here.start()

    def lead_there(which):
        return pltpu.make_async_remote_copy(
            src_ref=head, dst_ref=lead(which), send_sem=us.at[0], recv_sem=ur.at[0],
            device_id=twin, device_id_type=MESH)

    lead_there(core).start()
    for half in range(2):
        twin_send(0, half).start()

    ring_step(1)

    @pl.loop(1, NROW)
    def _(d):
        a_copy(d, (p + NROW - d) % NROW).wait_recv()

    def a_swap(which):
        return pltpu.make_async_remote_copy(
            src_ref=abuf.at[which], dst_ref=abuf.at[which], send_sem=us.at[1],
            recv_sem=ur.at[1], device_id=twin, device_id_type=MESH)

    a_swap(core).start()
    ring_step(2)
    a_swap(1 - core).wait_recv()

    row = lax.broadcasted_iota(jnp.int32, (256, 256), 0)
    col = lax.broadcasted_iota(jnp.int32, (256, 256), 1)
    row_order = one_hot(row == (col % 8) * NROW + col // 8)
    col_order = one_hot(col == (row % 16) * NCOL + ((row // 16) % 8) * 2 + row // 128)
    rows = pick_left(row_order, jnp.concatenate([abuf[0], abuf[1]], 1))
    sym[...] = jnp.where(
        row >= col, pick_right(rows, col_order), pick_left(col_order, rows, 0, 1))
    pick = one_hot(row[0:8] * NROW + p == col[0:8])
    h_ref[...] = pick_right(pick_left(pick, sym[...]), col_order, 1, 1)
    work[...] = sym[0:128, 0:128]

    @pl.loop(0, 2)
    def _(i):
        for k, v in enumerate(invert_factor([work[8 * k:8 * k + 8, :] for k in range(16)])):
            zd[i, 8 * k:8 * k + 8, :] = v

        @pl.when(i == 0)
        def _():
            low = mm(sym[128:256, 0:128], zd[0], 1, 1)
            work[...] = sym[128:256, 128:256] - mm(low, low, 1, 1)
            carry[...] = mm(low, zd[0])
            ring_step(3)

    ring_step(4)

    @pl.loop(1, NROW)
    def _(d):
        b_copy(d, (p + NROW - d) % NROW).wait_recv()

    zb[0:128, 0:128] = zd[0]
    zb[0:128, 128:256] = jnp.zeros((128, 128), jnp.float32)
    zb[128:256, 0:128] = -mm(zd[1], carry[...])
    zb[128:256, 128:256] = zd[1]
    inverse = pick_right(zb[...], col_order, 1, 1)
    cols = pick_right(bbuf[...], one_hot(col == (row % 128) * 2 + row // 128))
    own_cols = jnp.where(row == col * NCOL + q, 1.0, 0.0)
    t = jnp.where(col < 16, own_cols, mm(inverse, cols))
    w_ref[...] = mm(inverse, t, 0, 0)

    lead_there(1 - core).wait_recv()
    for half in range(2):
        for slot in range(8):
            twin_recv(slot, half).wait_recv()

    @pl.loop(1, 8)
    def _(d):
        head_copy(d, z).wait_send()

    @pl.loop(1, NROW)
    def _(d):
        a_copy(d, p).wait_send()
        b_copy(d, p).wait_send()

    for half in range(2):
        @pl.when(jnp.logical_not(to_self(half)))
        def _():
            scatter_send(half).wait_send()

    for half in range(2):
        for direction in range(2):
            for step in range(1, REACH[direction, half] + 1):
                ring_send(direction, step, half).wait_send()
        for slot in range(8):
            twin_send(slot, half).wait_send()
    lead_there(core).wait_send()
    a_swap(core).wait_send()
    lead_here.wait()
    own_here.wait()


def panel(x):
    dma = pltpu.SemaphoreType.DMA
    f32 = jnp.float32
    return pl.pallas_call(
        panel_kernel,
        out_shape=(
            jax.ShapeDtypeStruct((256, ROWS), f32),
            jax.ShapeDtypeStruct((256, 256), f32),
            jax.ShapeDtypeStruct((8, 256), f32),
        ),
        in_specs=[pl.BlockSpec(memory_space=pltpu.HBM)],
        out_specs=(
            pl.BlockSpec(memory_space=pltpu.HBM),
            pl.BlockSpec(memory_space=pltpu.VMEM),
            pl.BlockSpec(memory_space=pltpu.VMEM),
        ),
        scratch_shapes=[
            pltpu.VMEM((2 * ROWS, 128), f32),
            pltpu.VMEM((16, ROWS), f32),
            pltpu.VMEM((128, HEAD), f32),
            pltpu.VMEM((8, 128), f32),
            pltpu.VMEM((8, 256), f32),
            pltpu.VMEM((2, 256, 128), f32),
            pltpu.VMEM((256, 256), f32),
            pltpu.VMEM((256, 256), f32),
            pltpu.VMEM((128, 128), f32),
            pltpu.VMEM((128, 128), f32),
            pltpu.VMEM((2, 128, 128), f32),
            pltpu.VMEM((256, 256), f32),
            dma((2,)), dma((2,)),
            dma((8,)), dma((8,)),
            dma((2, 2, 5)), dma((2, 8)),
            dma((2, 8)), dma((2, 8)),
            dma((NROW,)), dma((NROW,)),
            dma((NROW,)), dma((NROW,)),
            dma((2,)), dma((2,)),
            dma((2,)), dma((2,)),
        ],
        compiler_params=pltpu.CompilerParams(
            collective_id=0, has_side_effects=True, vmem_limit_bytes=24 << 20),
        name="panel",
    )(pltpu.with_memory_space_constraint(x, pltpu.HBM))


def update_kernel(g_ref, w_ref, h_ref, x_ref, o_ref):
    p = lax.axis_index("row")
    q = lax.axis_index("col")
    size = g_ref.shape[1]
    first = pl.program_id(0) * size
    acc = lax.dot_general(
        g_ref[...], w_ref[...], (((0,), (0,)), ((), ())), precision=HIGH,
        preferred_element_type=jnp.float32)
    row = (first + lax.broadcasted_iota(jnp.int32, (size, 128), 0)) * NROW + p
    lane = lax.broadcasted_iota(jnp.int32, (size, 128), 1)
    left = jnp.where(lane < 16, acc[:, :128], x_ref[pl.ds(0, size, stride=2), :] - acc[:, :128])
    right = x_ref[pl.ds(1, size, stride=2), :] - acc[:, 128:]
    o_ref[pl.ds(0, size, stride=2), :] = jnp.where(row >= lane * NCOL + q, left, 0.0)
    o_ref[pl.ds(1, size, stride=2), :] = jnp.where(row >= (lane + 128) * NCOL + q, right, 0.0)

    @pl.when(pl.program_id(0) == 0)
    def _():
        keep = row[0:8] >= lane[0:8] * NCOL + q
        o_ref[pl.ds(0, 8, stride=2), :] = jnp.where(keep & (lane[0:8] < 16), mm(h_ref[...], w_ref[:, 0:128]), 0.0)


def update(g, w, h, x):
    size = 512
    return pl.pallas_call(
        update_kernel,
        grid=(ROWS // size,),
        out_shape=jax.ShapeDtypeStruct((2 * ROWS, 128), jnp.float32),
        in_specs=[
            pl.BlockSpec((256, size), lambda i: (0, i)),
            pl.BlockSpec((256, 256), lambda i: (0, 0)),
            pl.BlockSpec((8, 256), lambda i: (0, 0)),
            pl.BlockSpec((2 * size, 128), lambda i: (i, 0)),
        ],
        out_specs=pl.BlockSpec((2 * size, 128), lambda i: (i, 0)),
        compiler_params=pltpu.CompilerParams(vmem_limit_bytes=24 << 20),
        name="update",
    )(g, w, h, x)


def body(window):
    x = window.reshape(2 * ROWS, 128)
    g, w, h = panel(x)
    return update(g, w, h, x).reshape(1, ROWS, 1, COLS)


def solution(mesh):
    spec = P("row", None, "col", None)
    return jax.shard_map(body, mesh=mesh, in_specs=(spec,), out_specs=spec, check_vma=False)
```

```python
import jax
import jax.numpy as jnp
from jax import lax
from jax.experimental import pallas as pl
from jax.experimental.pallas import tpu as pltpu
from jax.sharding import PartitionSpec as P

MESH = pl.DeviceIdType.MESH
NROW = 32
NCOL = 16
ROWS = 2048
COLS = 256
HEAD = 128
STRIP = 256
HALF = ((128, 1024), (1152, 896))
REACH = {(0, 0): 4, (1, 0): 3, (0, 1): 3, (1, 1): 4}
SPOT = (12, 15)
HIGH = lax.Precision.HIGHEST


def mm(a, b, ca=1, cb=0):
    return lax.dot_general(a, b, (((ca,), (cb,)), ((), ())), precision=HIGH, preferred_element_type=jnp.float32)

def lane_bcast(v, c):
    return jnp.broadcast_to(v[:, c:c+1], (8, 128))

def sub_bcast(v, r):
    return jnp.broadcast_to(v[r:r+1, :], (8, 128))

def invert_factor(m, forward):
    lane = lax.broadcasted_iota(jnp.int32, (8, 128), 1)
    sub = lax.broadcasted_iota(jnp.int32, (8, 128), 0)
    m = list(m)
    out = []
    for j in range(16):
        if j in SPOT:
            forward(j)
        inside = (lane >= 8*j) & (lane < 8*j+8)
        own = [lane_bcast(m[j], 8*j+k) for k in range(8)]
        e = {(i, k): sub_bcast(own[k], i) for k in range(8) for i in range(k, 8)}
        r = []
        for k in range(8):
            rk = lax.rsqrt(e[k, k])
            r.append(rk)
            for i in range(k+1, 8):
                e[i, k] = e[i, k] * rk
            for c in range(k+1, 8):
                for i in range(c, 8):
                    e[i, c] = e[i, c] - e[i, k] * e[c, k]
        row = jnp.where(inside, jnp.where(lane == sub + 8*j, 1.0, 0.0), m[j])
        final = jnp.zeros((8, 128), jnp.float32)
        ups = []
        for k in range(8):
            u = sub_bcast(row, k) * r[k]
            ups.append(u)
            final = jnp.where(sub == k, u, final)
            if k < 7:
                l = own[k] * r[k]
                row = row - l * u
                for c in range(k+1, 8):
                    own[c] = own[c] - l * e[c, k]
        out.append(jnp.where(lane < 8*j+8, final, 0.0))
        for i in range(j+1, 16):
            d = [lane_bcast(m[i], 8*j+k) for k in range(8)]
            acc = jnp.where(inside, 0.0, m[i])
            for k in range(8):
                l = d[k] * r[k]
                acc = acc - l * ups[k]
                for c in range(k+1, 8):
                    d[c] = d[c] - l * e[c, k]
            m[i] = acc
    return out


def parts(v):
    high = v.astype(jnp.bfloat16)
    rest = v - high.astype(jnp.float32)
    middle = rest.astype(jnp.bfloat16)
    return high, middle, (rest - middle.astype(jnp.float32)).astype(jnp.bfloat16)


def one_hot(match):
    return jnp.where(match, 1.0, 0.0).astype(jnp.bfloat16)


def pick_left(chosen, v, ca=1, cb=0):
    return sum(
        lax.dot_general(chosen, part, (((ca,), (cb,)), ((), ())), preferred_element_type=jnp.float32)
        for part in parts(v))


def pick_right(v, chosen, ca=1, cb=0):
    return sum(
        lax.dot_general(part, chosen, (((ca,), (cb,)), ((), ())), preferred_element_type=jnp.float32)
        for part in parts(v))


def panel_kernel(
    x_ref, g_ref, w_ref, h_ref,
    xv, own, head, g8, b8, abuf, bbuf, sym, work, right, zd, inverse,
    xsem, osem, hs, hr, rs, rr, bs, br, as_, ar, ks, kr, ts, tr, us, ur,
):
    p = lax.axis_index("row")
    q = lax.axis_index("col")
    z = q // 2
    core = q % 2
    twin = (p, z * 2 + 1 - core)
    block = core * 16 + z * 2
    feeder = 2 * ((p % NCOL) // 2) + p // NCOL

    def to_self(half):
        return (block + half == p) & (p % NCOL == q)

    def from_self(h):
        return (q + 16 * h == p) & (feeder == q)

    barrier = pltpu.get_barrier_semaphore()

    @pl.loop(1, 8)
    def _(d):
        pl.semaphore_signal(
            barrier, inc=1, device_id=(p, ((z + d) % 8) * 2 + core), device_id_type=MESH)

    pl.semaphore_signal(barrier, inc=1, device_id=twin, device_id_type=MESH)

    @pl.loop(1, NROW)
    def _(d):
        pl.semaphore_signal(barrier, inc=1, device_id=((p + d) % NROW, q), device_id_type=MESH)

    waits = 7 + 1 + NROW - 1
    for half in range(2):
        @pl.when(jnp.logical_not(to_self(half)))
        def _():
            pl.semaphore_signal(
                barrier, inc=1, device_id=(block + half, p % NCOL), device_id_type=MESH)

        @pl.when(jnp.logical_not(from_self(half)))
        def _():
            pl.semaphore_signal(
                barrier, inc=1, device_id=(q + 16 * half, feeder), device_id_type=MESH)

        waits += jnp.where(to_self(half), 0, 1) + jnp.where(from_self(half), 0, 1)

    head_in = pltpu.make_async_copy(x_ref.at[pl.ds(0, 256)], xv.at[pl.ds(0, 256)], xsem.at[0])
    rest_in = pltpu.make_async_copy(x_ref.at[pl.ds(256, 3840)], xv.at[pl.ds(256, 3840)], xsem.at[1])
    head_in.start()
    rest_in.start()
    head_in.wait()
    own[:, 0:HEAD] = xv[pl.ds(0, HEAD, stride=2), :].T[0:16, :]
    head[pl.ds(pl.multiple_of(z * 16, 16), 16), :] = own[:, 0:HEAD]
    pl.semaphore_wait(barrier, waits)

    def head_copy(d, origin):
        rows = pl.ds(pl.multiple_of(origin * 16, 16), 16)
        return pltpu.make_async_remote_copy(
            src_ref=own.at[:, pl.ds(0, HEAD)], dst_ref=head.at[rows, :], send_sem=hs.at[d],
            recv_sem=hr.at[d], device_id=(p, ((z + d) % 8) * 2 + core), device_id_type=MESH)

    @pl.loop(1, 8)
    def _(d):
        head_copy(d, z).start()

    side = pl.ds(pl.multiple_of((p // NCOL) * HEAD, HEAD), HEAD)

    def scatter_send(half):
        return pltpu.make_async_remote_copy(
            src_ref=own.at[pl.ds(half * 8, 8), pl.ds(0, HEAD)], dst_ref=b8.at[:, side],
            send_sem=ts.at[half], recv_sem=tr.at[p // NCOL],
            device_id=(block + half, p % NCOL), device_id_type=MESH)

    def scatter_recv(h):
        lanes = b8.at[:, pl.ds(h * HEAD, HEAD)]
        return pltpu.make_async_remote_copy(
            src_ref=lanes, dst_ref=lanes, send_sem=ts.at[0], recv_sem=tr.at[h],
            device_id=(block, p % NCOL), device_id_type=MESH)

    for half in range(2):
        @pl.when(jnp.logical_not(to_self(half)))
        def _():
            scatter_send(half).start()

        @pl.when(to_self(half))
        def _():
            b8[:, side] = own[half * 8:half * 8 + 8, 0:HEAD]

    rest_in.wait()

    @pl.loop(1, 16)
    def _(b):
        lanes = pl.ds(pl.multiple_of(b * 128, 128), 128)
        own[:, lanes] = xv[pl.ds(b * 256, 128, stride=2), :].T[0:16, :]

    def piece(dist, half, which):
        rows = which * 128 + ((z + 8 - dist) % 8) * 16
        start, size = HALF[half]
        return g_ref.at[pl.ds(pl.multiple_of(rows, 16), 16), pl.ds(start, size)]

    def source(dist, half):
        start, size = HALF[half]
        return own.at[:, pl.ds(start, size)] if dist == 0 else piece(dist, half, core)

    def ring_send(direction, step, half):
        dist = step - 1 if direction == 0 else (9 - step) % 8
        slot = step if direction == 0 else 8 - step
        to = (z + 1) % 8 if direction == 0 else (z + 7) % 8
        return pltpu.make_async_remote_copy(
            src_ref=source(dist, half), dst_ref=piece(dist, half, core),
            send_sem=rs.at[direction, half, step], recv_sem=rr.at[half, slot],
            device_id=(p, to * 2 + core), device_id_type=MESH)

    def ring_recv(direction, step, half):
        slot = step if direction == 0 else 8 - step
        return pltpu.make_async_remote_copy(
            src_ref=piece(slot, half, core), dst_ref=piece(slot, half, core),
            send_sem=rs.at[direction, half, step], recv_sem=rr.at[half, slot],
            device_id=twin, device_id_type=MESH)

    def twin_send(slot, half):
        return pltpu.make_async_remote_copy(
            src_ref=source(slot, half), dst_ref=piece(slot, half, core),
            send_sem=bs.at[half, slot], recv_sem=br.at[half, slot],
            device_id=twin, device_id_type=MESH)

    def twin_recv(slot, half):
        return pltpu.make_async_remote_copy(
            src_ref=piece(slot, half, 1 - core), dst_ref=piece(slot, half, 1 - core),
            send_sem=bs.at[half, slot], recv_sem=br.at[half, slot],
            device_id=twin, device_id_type=MESH)

    def ring_step(step):
        for half in range(2):
            for direction in range(2):
                last = REACH[direction, half]
                if step <= last:
                    ring_recv(direction, step, half).wait_recv()
                    if step < last:
                        ring_send(direction, step + 1, half).start()
                    twin_send(step if direction == 0 else 8 - step, half).start()

    for half in range(2):
        ring_send(0, 1, half).start()
        ring_send(1, 1, half).start()

    @pl.loop(1, 8)
    def _(d):
        head_copy(d, (z + 8 - d) % 8).wait_recv()

    g8[...] = head[...].T[0:8, :]
    mine = pl.ds(pl.multiple_of(p * 8, 8), 8)
    abuf[core, mine, :] = g8[...]

    def shifted(d, sign):
        return ((p // 8 + 4 + sign * (d // 8)) % 4) * 8 + (p % 8 + 8 + sign * (d % 8)) % 8

    def a_copy(d, origin):
        rows = pl.ds(pl.multiple_of(origin * 8, 8), 8)
        return pltpu.make_async_remote_copy(
            src_ref=g8, dst_ref=abuf.at[core, rows, :], send_sem=as_.at[d], recv_sem=ar.at[d],
            device_id=(shifted(d, 1), q), device_id_type=MESH)

    @pl.loop(1, NROW)
    def _(d):
        a_copy(d, p).start()

    ring_step(1)
    for h in range(2):
        @pl.when(jnp.logical_not(from_self(h)))
        def _():
            scatter_recv(h).wait_recv()
    bbuf[mine, :] = b8[...]

    def b_copy(d, origin):
        rows = pl.ds(pl.multiple_of(origin * 8, 8), 8)
        return pltpu.make_async_remote_copy(
            src_ref=b8, dst_ref=bbuf.at[rows, :], send_sem=ks.at[d], recv_sem=kr.at[d],
            device_id=(shifted(d, 1), q), device_id_type=MESH)

    def lead(which):
        return g_ref.at[pl.ds(pl.multiple_of(which * 128, 128), 128), pl.ds(0, HEAD)]

    lead_here = pltpu.make_async_copy(head, lead(core), osem.at[0])
    lead_here.start()
    own_rows = pl.ds(pl.multiple_of(core * 128 + z * 16, 16), 16)
    own_here = pltpu.make_async_copy(
        own.at[:, pl.ds(HEAD, ROWS - HEAD)], g_ref.at[own_rows, pl.ds(HEAD, ROWS - HEAD)],
        osem.at[1])
    own_here.start()

    def lead_there(which):
        return pltpu.make_async_remote_copy(
            src_ref=head, dst_ref=lead(which), send_sem=us.at[0], recv_sem=ur.at[0],
            device_id=twin, device_id_type=MESH)

    lead_there(core).start()
    for half in range(2):
        twin_send(0, half).start()


    def a_swap(group, which):
        rows = pl.ds(pl.multiple_of(((p // 8 + 4 - group) % 4) * 64, 64), 64)
        return pltpu.make_async_remote_copy(
            src_ref=abuf.at[which, rows, :], dst_ref=abuf.at[which, rows, :],
            send_sem=us.at[1 + group], recv_sem=ur.at[1 + group], device_id=twin,
            device_id_type=MESH)

    for group in range(4):
        @pl.loop(max(1, group * 8), group * 8 + 8)
        def _(d):
            a_copy(d, shifted(d, -1)).wait_recv()

        a_swap(group, core).start()
    ring_step(2)

    @pl.loop(1, NROW)
    def _(d):
        b_copy(d, p).start()

    for group in range(4):
        a_swap(group, 1 - core).wait_recv()

    row = lax.broadcasted_iota(jnp.int32, (256, 256), 0)
    col = lax.broadcasted_iota(jnp.int32, (256, 256), 1)
    col_order = one_hot(col == (row % 16) * NCOL + ((row // 16) % 8) * 2 + row // 128)
    rows = jnp.concatenate([
        jnp.concatenate([abuf[c, pl.ds(k, NROW, stride=8), :] for k in range(8)], 0)
        for c in range(2)], 1)
    sym[...] = jnp.where(
        row >= col, pick_right(rows, col_order), pick_left(col_order, rows, 0, 1))
    work[...] = sym[0:128, 0:128]

    @pl.loop(0, 2)
    def _(i):
        def forward(j):
            @pl.when((i == 0) & (j == SPOT[0]))
            def _():
                ring_step(3)

            @pl.when((i == 1) & (j == SPOT[1]))
            def _():
                ring_step(4)

        blocks = invert_factor([work[8 * k:8 * k + 8, :] for k in range(16)], forward)
        for k, v in enumerate(blocks):
            zd[8 * k:8 * k + 8, :] = v

        @pl.when(i == 0)
        def _():
            low = mm(sym[128:256, 0:128], zd[...], 1, 1)
            work[...] = sym[128:256, 128:256] - mm(low, low, 1, 1)
            top = pick_right(zd[...], col_order[:, 0:128], 1, 1)
            inverse[0:128, :] = top
            right[...] = col_order[:, 128:256].astype(jnp.float32).T - mm(low, top)

    @pl.loop(1, NROW)
    def _(d):
        b_copy(d, shifted(d, -1)).wait_recv()

    inverse[128:256, :] = mm(zd[...], right[...])
    cols = pick_right(bbuf[...], one_hot(col == (row % 128) * 2 + row // 128))
    whole = pair(inverse[...])
    own_cols = jnp.where(row == col * NCOL + q, 1.0, 0.0)
    t = jnp.where(col < 16, own_cols, dot3(whole, pair(cols)))
    w_ref[...] = dot3(whole, pair(t), 0, 0)
    pick = one_hot(row[0:8] * NROW + p == col[0:8])
    h_ref[...] = pick_right(pick_left(pick, sym[...]), col_order, 1, 1)

    lead_there(1 - core).wait_recv()
    for half in range(2):
        for slot in range(8):
            twin_recv(slot, half).wait_recv()

    @pl.loop(1, 8)
    def _(d):
        head_copy(d, z).wait_send()

    @pl.loop(1, NROW)
    def _(d):
        a_copy(d, p).wait_send()
        b_copy(d, p).wait_send()

    for half in range(2):
        @pl.when(jnp.logical_not(to_self(half)))
        def _():
            scatter_send(half).wait_send()

    for half in range(2):
        for direction in range(2):
            for step in range(1, REACH[direction, half] + 1):
                ring_send(direction, step, half).wait_send()
        for slot in range(8):
            twin_send(slot, half).wait_send()
    lead_there(core).wait_send()
    for group in range(4):
        a_swap(group, core).wait_send()
    lead_here.wait()
    own_here.wait()


def panel(x):
    dma = pltpu.SemaphoreType.DMA
    f32 = jnp.float32
    return pl.pallas_call(
        panel_kernel,
        out_shape=(
            jax.ShapeDtypeStruct((256, ROWS), f32),
            jax.ShapeDtypeStruct((256, 256), f32),
            jax.ShapeDtypeStruct((8, 256), f32),
        ),
        in_specs=[pl.BlockSpec(memory_space=pltpu.HBM)],
        out_specs=(
            pl.BlockSpec(memory_space=pltpu.HBM),
            pl.BlockSpec(memory_space=pltpu.VMEM),
            pl.BlockSpec(memory_space=pltpu.VMEM),
        ),
        scratch_shapes=[
            pltpu.VMEM((2 * ROWS, 128), f32),
            pltpu.VMEM((16, ROWS), f32),
            pltpu.VMEM((128, HEAD), f32),
            pltpu.VMEM((8, 128), f32),
            pltpu.VMEM((8, 256), f32),
            pltpu.VMEM((2, 256, 128), f32),
            pltpu.VMEM((256, 256), f32),
            pltpu.VMEM((256, 256), f32),
            pltpu.VMEM((128, 128), f32),
            pltpu.VMEM((128, 256), f32),
            pltpu.VMEM((128, 128), f32),
            pltpu.VMEM((256, 256), f32),
            dma((2,)), dma((2,)),
            dma((8,)), dma((8,)),
            dma((2, 2, 5)), dma((2, 8)),
            dma((2, 8)), dma((2, 8)),
            dma((NROW,)), dma((NROW,)),
            dma((NROW,)), dma((NROW,)),
            dma((2,)), dma((2,)),
            dma((5,)), dma((5,)),
        ],
        compiler_params=pltpu.CompilerParams(
            collective_id=0, has_side_effects=True, vmem_limit_bytes=24 << 20),
        name="panel",
    )(pltpu.with_memory_space_constraint(x, pltpu.HBM))


def pair(v):
    high = v.astype(jnp.bfloat16)
    return high, (v - high.astype(jnp.float32)).astype(jnp.bfloat16)


def dot3(a, b, ca=1, cb=0):
    def one(u, v):
        return lax.dot_general(
            u, v, (((ca,), (cb,)), ((), ())), preferred_element_type=jnp.float32)

    return one(a[0], b[0]) + (one(a[0], b[1]) + one(a[1], b[0]))


def update_kernel(g_ref, w_ref, h_ref, x_ref, o_ref, ov, sem):
    p = lax.axis_index("row")
    q = lax.axis_index("col")
    size = STRIP
    weights = pair(w_ref[...])
    copies = []
    for t in range(ROWS // size):
        acc = dot3(pair(g_ref[:, t * size:(t + 1) * size]), weights, 0, 0)
        start = 2 * t * size
        row = (t * size + lax.broadcasted_iota(jnp.int32, (size, 128), 0)) * NROW + p
        lane = lax.broadcasted_iota(jnp.int32, (size, 128), 1)
        left = jnp.where(
            lane < 16, acc[:, :128], x_ref[pl.ds(start, size, stride=2), :] - acc[:, :128])
        right = x_ref[pl.ds(start + 1, size, stride=2), :] - acc[:, 128:]
        if t * size * NROW < COLS * NCOL:
            left = jnp.where(row >= lane * NCOL + q, left, 0.0)
            right = jnp.where(row >= (lane + 128) * NCOL + q, right, 0.0)
        ov[pl.ds(start, size, stride=2), :] = left
        ov[pl.ds(start + 1, size, stride=2), :] = right
        if t == 0:
            keep = (row[0:8] >= lane[0:8] * NCOL + q) & (lane[0:8] < 16)
            ov[pl.ds(0, 8, stride=2), :] = jnp.where(
                keep, mm(h_ref[...], w_ref[:, 0:128]), 0.0)
        copies.append(pltpu.make_async_copy(
            ov.at[pl.ds(start, 2 * size)], o_ref.at[pl.ds(start, 2 * size)], sem.at[t]))
        copies[-1].start()
    for copy in copies:
        copy.wait()


def update(g, w, h, x):
    vmem = pl.BlockSpec(memory_space=pltpu.VMEM)
    return pl.pallas_call(
        update_kernel,
        out_shape=jax.ShapeDtypeStruct((2 * ROWS, 128), jnp.float32),
        in_specs=[vmem, vmem, vmem, vmem],
        out_specs=pl.BlockSpec(memory_space=pltpu.HBM),
        scratch_shapes=[
            pltpu.VMEM((2 * ROWS, 128), jnp.float32), pltpu.SemaphoreType.DMA((ROWS // STRIP,))],
        compiler_params=pltpu.CompilerParams(vmem_limit_bytes=24 << 20),
        name="update",
    )(g, w, h, x)


def body(window):
    x = window.reshape(2 * ROWS, 128)
    g, w, h = panel(x)
    return update(g, w, h, x).reshape(1, ROWS, 1, COLS)


def solution(mesh):
    spec = P("row", None, "col", None)
    return jax.shard_map(body, mesh=mesh, in_specs=(spec,), out_specs=spec, check_vma=False)
```

```python
import jax
import jax.numpy as jnp
from jax import lax
from jax.experimental import pallas as pl
from jax.experimental.pallas import tpu as pltpu
from jax.sharding import PartitionSpec as P

MESH = pl.DeviceIdType.MESH
NROW = 32
NCOL = 16
ROWS = 2048
COLS = 256
HEAD = 128
STRIP = 256
HALF = ((128, 1024), (1152, 896))
REACH = {(0, 0): 4, (1, 0): 3, (0, 1): 3, (1, 1): 4}
SPOT = (12, 15)
HIGH = lax.Precision.HIGHEST


def mm(a, b, ca=1, cb=0):
    return lax.dot_general(a, b, (((ca,), (cb,)), ((), ())), precision=HIGH, preferred_element_type=jnp.float32)

def lane_bcast(v, c):
    return jnp.broadcast_to(v[:, c:c+1], (8, 128))

def sub_bcast(v, r):
    return jnp.broadcast_to(v[r:r+1, :], (8, 128))

def invert_factor(m, forward):
    lane = lax.broadcasted_iota(jnp.int32, (8, 128), 1)
    sub = lax.broadcasted_iota(jnp.int32, (8, 128), 0)
    m = list(m)
    out = []
    for j in range(16):
        if j in SPOT:
            forward(j)
        inside = (lane >= 8*j) & (lane < 8*j+8)
        own = [lane_bcast(m[j], 8*j+k) for k in range(8)]
        e = {(i, k): sub_bcast(own[k], i) for k in range(8) for i in range(k, 8)}
        r = []
        for k in range(8):
            rk = lax.rsqrt(e[k, k])
            r.append(rk)
            for i in range(k+1, 8):
                e[i, k] = e[i, k] * rk
            for c in range(k+1, 8):
                for i in range(c, 8):
                    e[i, c] = e[i, c] - e[i, k] * e[c, k]
        row = jnp.where(inside, jnp.where(lane == sub + 8*j, 1.0, 0.0), m[j])
        final = jnp.zeros((8, 128), jnp.float32)
        ups = []
        for k in range(8):
            u = sub_bcast(row, k) * r[k]
            ups.append(u)
            final = jnp.where(sub == k, u, final)
            if k < 7:
                l = own[k] * r[k]
                row = row - l * u
                for c in range(k+1, 8):
                    own[c] = own[c] - l * e[c, k]
        out.append(jnp.where(lane < 8*j+8, final, 0.0))
        for i in range(j+1, 16):
            d = [lane_bcast(m[i], 8*j+k) for k in range(8)]
            acc = jnp.where(inside, 0.0, m[i])
            for k in range(8):
                l = d[k] * r[k]
                acc = acc - l * ups[k]
                for c in range(k+1, 8):
                    d[c] = d[c] - l * e[c, k]
            m[i] = acc
    return out


def parts(v):
    high = v.astype(jnp.bfloat16)
    rest = v - high.astype(jnp.float32)
    middle = rest.astype(jnp.bfloat16)
    return high, middle, (rest - middle.astype(jnp.float32)).astype(jnp.bfloat16)


def one_hot(match):
    return jnp.where(match, 1.0, 0.0).astype(jnp.bfloat16)


def pick_left(chosen, v, ca=1, cb=0):
    return sum(
        lax.dot_general(chosen, part, (((ca,), (cb,)), ((), ())), preferred_element_type=jnp.float32)
        for part in parts(v))


def pick_right(v, chosen, ca=1, cb=0):
    return sum(
        lax.dot_general(part, chosen, (((ca,), (cb,)), ((), ())), preferred_element_type=jnp.float32)
        for part in parts(v))


def panel_kernel(
    x_ref, g_ref, w_ref, h_ref,
    xv, own, head, g8, b8, abuf, bbuf, sym, work, right, zd, inverse, below, first, late_order,
    xsem, osem, hs, hr, rs, rr, bs, br, as_, ar, ks, kr, ts, tr, us, ur,
):
    p = lax.axis_index("row")
    q = lax.axis_index("col")
    z = q // 2
    core = q % 2
    twin = (p, z * 2 + 1 - core)
    block = core * 16 + z * 2
    feeder = 2 * ((p % NCOL) // 2) + p // NCOL

    def to_self(half):
        return (block + half == p) & (p % NCOL == q)

    def from_self(h):
        return (q + 16 * h == p) & (feeder == q)

    head_in = pltpu.make_async_copy(x_ref.at[pl.ds(0, 256)], xv.at[pl.ds(0, 256)], xsem.at[0])
    rest_in = pltpu.make_async_copy(x_ref.at[pl.ds(256, 3840)], xv.at[pl.ds(256, 3840)], xsem.at[1])
    head_in.start()
    rest_in.start()

    firsts = [lax.rem(p // 8 + i, 4) * 8 for i in range(4)]
    seconds = [lax.rem(p % 8 + j, 8) for j in range(8)]
    row_peers = [(firsts[d // 8] + seconds[d % 8], q) for d in range(1, NROW)]
    z_peers = [(p, lax.rem(z + d, 8) * 2 + core) for d in range(1, 8)]

    barrier = pltpu.get_barrier_semaphore()
    for peer in z_peers + [twin] + row_peers:
        pl.semaphore_signal(barrier, inc=1, device_id=peer, device_id_type=MESH)

    waits = 7 + 1 + NROW - 1
    for half in range(2):
        @pl.when(jnp.logical_not(to_self(half)))
        def _():
            pl.semaphore_signal(
                barrier, inc=1, device_id=(block + half, p % NCOL), device_id_type=MESH)

        @pl.when(jnp.logical_not(from_self(half)))
        def _():
            pl.semaphore_signal(
                barrier, inc=1, device_id=(q + 16 * half, feeder), device_id_type=MESH)

        waits += jnp.where(to_self(half), 0, 1) + jnp.where(from_self(half), 0, 1)

    head_in.wait()
    own[:, 0:HEAD] = xv[pl.ds(0, HEAD, stride=2), :].T[0:16, :]
    head[pl.ds(pl.multiple_of(z * 16, 16), 16), :] = own[:, 0:HEAD]
    pl.semaphore_wait(barrier, waits)

    z_rows = pl.ds(pl.multiple_of(z * 16, 16), 16)
    head_sends = [
        pltpu.make_async_remote_copy(
            src_ref=own.at[:, pl.ds(0, HEAD)], dst_ref=head.at[z_rows, :], send_sem=hs.at[0],
            recv_sem=hr.at[0], device_id=peer, device_id_type=MESH)
        for peer in z_peers]
    for copy in head_sends:
        copy.start()

    def bulk(ref, send_sem, recv_sem):
        return pltpu.make_async_remote_copy(
            src_ref=ref, dst_ref=ref, send_sem=send_sem, recv_sem=recv_sem, device_id=twin,
            device_id_type=MESH)

    heads = bulk(head.at[pl.ds(0, 112), :], hs.at[0], hr.at[0])

    side = pl.ds(pl.multiple_of((p // NCOL) * HEAD, HEAD), HEAD)

    def scatter_send(half):
        return pltpu.make_async_remote_copy(
            src_ref=own.at[pl.ds(half * 8, 8), pl.ds(0, HEAD)], dst_ref=b8.at[:, side],
            send_sem=ts.at[half], recv_sem=tr.at[p // NCOL],
            device_id=(block + half, p % NCOL), device_id_type=MESH)

    def scatter_recv(h):
        lanes = b8.at[:, pl.ds(h * HEAD, HEAD)]
        return pltpu.make_async_remote_copy(
            src_ref=lanes, dst_ref=lanes, send_sem=ts.at[0], recv_sem=tr.at[h],
            device_id=(block, p % NCOL), device_id_type=MESH)

    for half in range(2):
        @pl.when(jnp.logical_not(to_self(half)))
        def _():
            scatter_send(half).start()

        @pl.when(to_self(half))
        def _():
            b8[:, side] = own[half * 8:half * 8 + 8, 0:HEAD]

    rest_in.wait()

    @pl.loop(1, 16)
    def _(b):
        lanes = pl.ds(pl.multiple_of(b * 128, 128), 128)
        own[:, lanes] = xv[pl.ds(b * 256, 128, stride=2), :].T[0:16, :]

    def piece(dist, half, which):
        rows = which * 128 + ((z + 8 - dist) % 8) * 16
        start, size = HALF[half]
        return g_ref.at[pl.ds(pl.multiple_of(rows, 16), 16), pl.ds(start, size)]

    def source(dist, half):
        start, size = HALF[half]
        return own.at[:, pl.ds(start, size)] if dist == 0 else piece(dist, half, core)

    def ring_send(direction, step, half):
        dist = step - 1 if direction == 0 else (9 - step) % 8
        slot = step if direction == 0 else 8 - step
        to = (z + 1) % 8 if direction == 0 else (z + 7) % 8
        return pltpu.make_async_remote_copy(
            src_ref=source(dist, half), dst_ref=piece(dist, half, core),
            send_sem=rs.at[direction, half, step], recv_sem=rr.at[half, slot],
            device_id=(p, to * 2 + core), device_id_type=MESH)

    def ring_recv(direction, step, half):
        slot = step if direction == 0 else 8 - step
        return pltpu.make_async_remote_copy(
            src_ref=piece(slot, half, core), dst_ref=piece(slot, half, core),
            send_sem=rs.at[direction, half, step], recv_sem=rr.at[half, slot],
            device_id=twin, device_id_type=MESH)

    def twin_send(slot, half):
        return pltpu.make_async_remote_copy(
            src_ref=source(slot, half), dst_ref=piece(slot, half, core),
            send_sem=bs.at[half, slot], recv_sem=br.at[half, slot],
            device_id=twin, device_id_type=MESH)

    def twin_recv(slot, half):
        return pltpu.make_async_remote_copy(
            src_ref=piece(slot, half, 1 - core), dst_ref=piece(slot, half, 1 - core),
            send_sem=bs.at[half, slot], recv_sem=br.at[half, slot],
            device_id=twin, device_id_type=MESH)

    def ring_step(step):
        for half in range(2):
            for direction in range(2):
                last = REACH[direction, half]
                if step <= last:
                    ring_recv(direction, step, half).wait_recv()
                    if step < last:
                        ring_send(direction, step + 1, half).start()
                    twin_send(step if direction == 0 else 8 - step, half).start()

    for half in range(2):
        ring_send(0, 1, half).start()
        ring_send(1, 1, half).start()

    heads.wait_recv()

    g8[...] = head[...].T[0:8, :]
    mine = pl.ds(pl.multiple_of(p * 8, 8), 8)
    abuf[core, mine, :] = g8[...]

    for d in range(1, NROW):
        pltpu.make_async_remote_copy(
            src_ref=g8, dst_ref=abuf.at[core, mine, :], send_sem=as_.at[0],
            recv_sem=ar.at[d // 8], device_id=row_peers[d - 1], device_id_type=MESH).start()

    ring_step(1)
    for h in range(2):
        @pl.when(jnp.logical_not(from_self(h)))
        def _():
            scatter_recv(h).wait_recv()
    bbuf[mine, :] = b8[...]

    def lead(which):
        return g_ref.at[pl.ds(pl.multiple_of(which * 128, 128), 128), pl.ds(0, HEAD)]

    lead_here = pltpu.make_async_copy(head, lead(core), osem.at[0])
    lead_here.start()
    own_rows = pl.ds(pl.multiple_of(core * 128 + z * 16, 16), 16)
    own_here = pltpu.make_async_copy(
        own.at[:, pl.ds(HEAD, ROWS - HEAD)], g_ref.at[own_rows, pl.ds(HEAD, ROWS - HEAD)],
        osem.at[1])
    own_here.start()

    def lead_there(which):
        return pltpu.make_async_remote_copy(
            src_ref=head, dst_ref=lead(which), send_sem=us.at[0], recv_sem=ur.at[0],
            device_id=twin, device_id_type=MESH)

    lead_there(core).start()
    for half in range(2):
        twin_send(0, half).start()


    def a_swap(group, which):
        rows = pl.ds(pl.multiple_of(((p // 8 + 4 - group) % 4) * 64, 64), 64)
        return pltpu.make_async_remote_copy(
            src_ref=abuf.at[which, rows, :], dst_ref=abuf.at[which, rows, :],
            send_sem=us.at[1 + group], recv_sem=ur.at[1 + group], device_id=twin,
            device_id_type=MESH)

    for group in range(4):
        count = 56 if group == 0 else 64
        bulk(abuf.at[core, pl.ds(0, count), :], as_.at[0], ar.at[group]).wait_recv()
        a_swap(group, core).start()
    ring_step(2)

    for peer in row_peers:
        pltpu.make_async_remote_copy(
            src_ref=b8, dst_ref=bbuf.at[mine, :], send_sem=ks.at[0], recv_sem=kr.at[0],
            device_id=peer, device_id_type=MESH).start()
    b_all = bulk(bbuf.at[pl.ds(0, 248), :], ks.at[0], kr.at[0])

    for group in range(4):
        a_swap(group, 1 - core).wait_recv()

    row = lax.broadcasted_iota(jnp.int32, (256, 256), 0)
    col = lax.broadcasted_iota(jnp.int32, (256, 256), 1)
    col_order = one_hot(col == (row % 16) * NCOL + ((row // 16) % 8) * 2 + row // 128)
    rows = jnp.concatenate([
        jnp.concatenate([abuf[c, pl.ds(k, NROW, stride=8), :] for k in range(8)], 0)
        for c in range(2)], 1)
    sym[...] = jnp.where(
        row >= col, pick_right(rows, col_order), pick_left(col_order, rows, 0, 1))
    work[...] = sym[0:128, 0:128]
    late_order[...] = col_order[:, 128:256].astype(jnp.float32).T

    below[...] = jnp.zeros((128, 128), jnp.float32)
    first[...] = jnp.zeros((128, 128), jnp.float32)

    @pl.loop(0, 2)
    def _(i):
        top = pick_right(first[...], col_order[:, 0:128], 1, 1)
        inverse[0:128, :] = top
        right[...] = late_order[...] - mm(below[...], top)

        def forward(j):
            @pl.when((i == 0) & (j == SPOT[0]))
            def _():
                ring_step(3)

            @pl.when((i == 1) & (j == SPOT[1]))
            def _():
                ring_step(4)

        blocks = invert_factor([work[8 * k:8 * k + 8, :] for k in range(16)], forward)
        for k, v in enumerate(blocks):
            zd[8 * k:8 * k + 8, :] = v

        @pl.when(i == 0)
        def _():
            low = mm(sym[128:256, 0:128], zd[...], 1, 1)
            work[...] = sym[128:256, 128:256] - mm(low, low, 1, 1)
            below[...] = low
            first[...] = zd[...]

    b_all.wait_recv()

    inverse[128:256, :] = mm(zd[...], right[...])
    cols = pick_right(bbuf[...], one_hot(col == (row % 128) * 2 + row // 128))
    whole = pair(inverse[...])
    own_cols = jnp.where(row == col * NCOL + q, 1.0, 0.0)
    t = jnp.where(col < 16, own_cols, dot3(whole, pair(cols)))
    w_ref[...] = dot3(whole, pair(t), 0, 0)
    pick = one_hot(row[0:8] * NROW + p == col[0:8])
    h_ref[...] = pick_right(pick_left(pick, sym[...]), col_order, 1, 1)

    lead_there(1 - core).wait_recv()
    for half in range(2):
        for slot in range(8):
            twin_recv(slot, half).wait_recv()

    heads.wait_send()

    bulk(abuf.at[core, pl.ds(0, 248), :], as_.at[0], ar.at[0]).wait_send()
    b_all.wait_send()

    for half in range(2):
        @pl.when(jnp.logical_not(to_self(half)))
        def _():
            scatter_send(half).wait_send()

    for half in range(2):
        for direction in range(2):
            for step in range(1, REACH[direction, half] + 1):
                ring_send(direction, step, half).wait_send()
        for slot in range(8):
            twin_send(slot, half).wait_send()
    lead_there(core).wait_send()
    for group in range(4):
        a_swap(group, core).wait_send()
    lead_here.wait()
    own_here.wait()


def panel(x):
    dma = pltpu.SemaphoreType.DMA
    f32 = jnp.float32
    return pl.pallas_call(
        panel_kernel,
        out_shape=(
            jax.ShapeDtypeStruct((256, ROWS), f32),
            jax.ShapeDtypeStruct((256, 256), f32),
            jax.ShapeDtypeStruct((8, 256), f32),
        ),
        in_specs=[pl.BlockSpec(memory_space=pltpu.HBM)],
        out_specs=(
            pl.BlockSpec(memory_space=pltpu.HBM),
            pl.BlockSpec(memory_space=pltpu.VMEM),
            pl.BlockSpec(memory_space=pltpu.VMEM),
        ),
        scratch_shapes=[
            pltpu.VMEM((2 * ROWS, 128), f32),
            pltpu.VMEM((16, ROWS), f32),
            pltpu.VMEM((128, HEAD), f32),
            pltpu.VMEM((8, 128), f32),
            pltpu.VMEM((8, 256), f32),
            pltpu.VMEM((2, 256, 128), f32),
            pltpu.VMEM((256, 256), f32),
            pltpu.VMEM((256, 256), f32),
            pltpu.VMEM((128, 128), f32),
            pltpu.VMEM((128, 256), f32),
            pltpu.VMEM((128, 128), f32),
            pltpu.VMEM((256, 256), f32),
            pltpu.VMEM((128, 128), f32),
            pltpu.VMEM((128, 128), f32),
            pltpu.VMEM((128, 256), f32),
            dma((2,)), dma((2,)),
            dma((1,)), dma((1,)),
            dma((2, 2, 5)), dma((2, 8)),
            dma((2, 8)), dma((2, 8)),
            dma((1,)), dma((4,)),
            dma((1,)), dma((1,)),
            dma((2,)), dma((2,)),
            dma((5,)), dma((5,)),
        ],
        compiler_params=pltpu.CompilerParams(
            collective_id=0, has_side_effects=True, vmem_limit_bytes=24 << 20),
        name="panel",
    )(pltpu.with_memory_space_constraint(x, pltpu.HBM))


def pair(v):
    high = v.astype(jnp.bfloat16)
    return high, (v - high.astype(jnp.float32)).astype(jnp.bfloat16)


def dot3(a, b, ca=1, cb=0):
    def one(u, v):
        return lax.dot_general(
            u, v, (((ca,), (cb,)), ((), ())), preferred_element_type=jnp.float32)

    return one(a[0], b[0]) + (one(a[0], b[1]) + one(a[1], b[0]))


def update_kernel(g_ref, w_ref, h_ref, x_ref, o_ref, ov, sem):
    p = lax.axis_index("row")
    q = lax.axis_index("col")
    size = STRIP
    weights = pair(w_ref[...])
    copies = []
    for t in range(ROWS // size):
        acc = dot3(pair(g_ref[:, t * size:(t + 1) * size]), weights, 0, 0)
        start = 2 * t * size
        row = (t * size + lax.broadcasted_iota(jnp.int32, (size, 128), 0)) * NROW + p
        lane = lax.broadcasted_iota(jnp.int32, (size, 128), 1)
        left = jnp.where(
            lane < 16, acc[:, :128], x_ref[pl.ds(start, size, stride=2), :] - acc[:, :128])
        right = x_ref[pl.ds(start + 1, size, stride=2), :] - acc[:, 128:]
        if t * size * NROW < COLS * NCOL:
            left = jnp.where(row >= lane * NCOL + q, left, 0.0)
            right = jnp.where(row >= (lane + 128) * NCOL + q, right, 0.0)
        ov[pl.ds(start, size, stride=2), :] = left
        ov[pl.ds(start + 1, size, stride=2), :] = right
        if t == 0:
            keep = (row[0:8] >= lane[0:8] * NCOL + q) & (lane[0:8] < 16)
            ov[pl.ds(0, 8, stride=2), :] = jnp.where(
                keep, mm(h_ref[...], w_ref[:, 0:128]), 0.0)
        copies.append(pltpu.make_async_copy(
            ov.at[pl.ds(start, 2 * size)], o_ref.at[pl.ds(start, 2 * size)], sem.at[t]))
        copies[-1].start()
    for copy in copies:
        copy.wait()


def update(g, w, h, x):
    vmem = pl.BlockSpec(memory_space=pltpu.VMEM)
    return pl.pallas_call(
        update_kernel,
        out_shape=jax.ShapeDtypeStruct((2 * ROWS, 128), jnp.float32),
        in_specs=[vmem, vmem, vmem, vmem],
        out_specs=pl.BlockSpec(memory_space=pltpu.HBM),
        scratch_shapes=[
            pltpu.VMEM((2 * ROWS, 128), jnp.float32), pltpu.SemaphoreType.DMA((ROWS // STRIP,))],
        compiler_params=pltpu.CompilerParams(vmem_limit_bytes=24 << 20),
        name="update",
    )(g, w, h, x)


def body(window):
    x = window.reshape(2 * ROWS, 128)
    g, w, h = panel(x)
    return update(g, w, h, x).reshape(1, ROWS, 1, COLS)


def solution(mesh):
    spec = P("row", None, "col", None)
    return jax.shard_map(body, mesh=mesh, in_specs=(spec,), out_specs=spec, check_vma=False)
```

```python
import jax
import jax.numpy as jnp
from jax import lax
from jax.experimental import pallas as pl
from jax.experimental.pallas import tpu as pltpu
from jax.sharding import PartitionSpec as P

MESH = pl.DeviceIdType.MESH
NROW = 32
NCOL = 16
ROWS = 2048
COLS = 256
HEAD = 128
STRIP = 256
HALF = ((128, 1024), (1152, 896))
FIRST_ORDER = (2, 1, 3, 0)
SECOND_ORDER = (4, 3, 5, 2, 6, 1, 7, 0)
REACH = {(0, 0): 4, (1, 0): 3, (0, 1): 3, (1, 1): 4}
SPOT = (12, 15)
HIGH = lax.Precision.HIGHEST


def mm(a, b, ca=1, cb=0):
    return lax.dot_general(a, b, (((ca,), (cb,)), ((), ())), precision=HIGH, preferred_element_type=jnp.float32)

def lane_bcast(v, c):
    return jnp.broadcast_to(v[:, c:c+1], (8, 128))

def sub_bcast(v, r):
    return jnp.broadcast_to(v[r:r+1, :], (8, 128))

def invert_factor(m, forward):
    lane = lax.broadcasted_iota(jnp.int32, (8, 128), 1)
    sub = lax.broadcasted_iota(jnp.int32, (8, 128), 0)
    m = list(m)
    out = []
    for j in range(16):
        if j in SPOT:
            forward(j)
        inside = (lane >= 8*j) & (lane < 8*j+8)
        own = [lane_bcast(m[j], 8*j+k) for k in range(8)]
        e = {(i, k): sub_bcast(own[k], i) for k in range(8) for i in range(k, 8)}
        r = []
        for k in range(8):
            rk = lax.rsqrt(e[k, k])
            r.append(rk)
            for i in range(k+1, 8):
                e[i, k] = e[i, k] * rk
            for c in range(k+1, 8):
                for i in range(c, 8):
                    e[i, c] = e[i, c] - e[i, k] * e[c, k]
        row = jnp.where(inside, jnp.where(lane == sub + 8*j, 1.0, 0.0), m[j])
        final = jnp.zeros((8, 128), jnp.float32)
        ups = []
        for k in range(8):
            u = sub_bcast(row, k) * r[k]
            ups.append(u)
            final = jnp.where(sub == k, u, final)
            if k < 7:
                l = own[k] * r[k]
                row = row - l * u
                for c in range(k+1, 8):
                    own[c] = own[c] - l * e[c, k]
        out.append(jnp.where(lane < 8*j+8, final, 0.0))
        for i in range(j+1, 16):
            d = [lane_bcast(m[i], 8*j+k) for k in range(8)]
            acc = jnp.where(inside, 0.0, m[i])
            for k in range(8):
                l = d[k] * r[k]
                acc = acc - l * ups[k]
                for c in range(k+1, 8):
                    d[c] = d[c] - l * e[c, k]
            m[i] = acc
    return out


def parts(v):
    high = v.astype(jnp.bfloat16)
    rest = v - high.astype(jnp.float32)
    middle = rest.astype(jnp.bfloat16)
    return high, middle, (rest - middle.astype(jnp.float32)).astype(jnp.bfloat16)


def one_hot(match):
    return jnp.where(match, 1.0, 0.0).astype(jnp.bfloat16)


def pick_left(chosen, v, ca=1, cb=0):
    return sum(
        lax.dot_general(chosen, part, (((ca,), (cb,)), ((), ())), preferred_element_type=jnp.float32)
        for part in parts(v))


def pick_right(v, chosen, ca=1, cb=0):
    return sum(
        lax.dot_general(part, chosen, (((ca,), (cb,)), ((), ())), preferred_element_type=jnp.float32)
        for part in parts(v))


def panel_kernel(
    x_ref, g_ref, w_ref, h_ref,
    xv, own, head, g8, b8, abuf, bbuf, sym, work, right, zd, inverse, below, first, late_order,
    xsem, osem, hs, hr, rs, rr, bs, br, as_, ar, ks, kr, ts, tr, us, ur,
):
    p = lax.axis_index("row")
    q = lax.axis_index("col")
    z = q // 2
    core = q % 2
    twin = (p, z * 2 + 1 - core)
    block = core * 16 + z * 2
    feeder = 2 * ((p % NCOL) // 2) + p // NCOL

    def to_self(half):
        return (block + half == p) & (p % NCOL == q)

    def from_self(h):
        return (q + 16 * h == p) & (feeder == q)

    head_in = pltpu.make_async_copy(x_ref.at[pl.ds(0, 256)], xv.at[pl.ds(0, 256)], xsem.at[0])
    rest_in = pltpu.make_async_copy(x_ref.at[pl.ds(256, 3840)], xv.at[pl.ds(256, 3840)], xsem.at[1])
    head_in.start()
    rest_in.start()

    firsts = [lax.rem(p // 8 + i, 4) * 8 for i in range(4)]
    seconds = [lax.rem(p % 8 + j, 8) for j in range(8)]
    steps = [(i, j) for i in FIRST_ORDER for j in SECOND_ORDER if i + j > 0]
    row_peers = [(firsts[i] + seconds[j], q) for i, j in steps]
    z_peers = [(p, lax.rem(z + j, 8) * 2 + core) for j in SECOND_ORDER if j > 0]

    barrier = pltpu.get_barrier_semaphore()
    for peer in z_peers + [twin] + row_peers:
        pl.semaphore_signal(barrier, inc=1, device_id=peer, device_id_type=MESH)

    waits = 7 + 1 + NROW - 1
    for half in range(2):
        @pl.when(jnp.logical_not(to_self(half)))
        def _():
            pl.semaphore_signal(
                barrier, inc=1, device_id=(block + half, p % NCOL), device_id_type=MESH)

        @pl.when(jnp.logical_not(from_self(half)))
        def _():
            pl.semaphore_signal(
                barrier, inc=1, device_id=(q + 16 * half, feeder), device_id_type=MESH)

        waits += jnp.where(to_self(half), 0, 1) + jnp.where(from_self(half), 0, 1)

    head_in.wait()
    own[:, 0:HEAD] = xv[pl.ds(0, HEAD, stride=2), :].T[0:16, :]
    head[pl.ds(pl.multiple_of(z * 16, 16), 16), :] = own[:, 0:HEAD]
    pl.semaphore_wait(barrier, waits)

    z_rows = pl.ds(pl.multiple_of(z * 16, 16), 16)
    head_sends = [
        pltpu.make_async_remote_copy(
            src_ref=own.at[:, pl.ds(0, HEAD)], dst_ref=head.at[z_rows, :], send_sem=hs.at[0],
            recv_sem=hr.at[0], device_id=peer, device_id_type=MESH)
        for peer in z_peers]
    for copy in head_sends:
        copy.start()

    def bulk(ref, send_sem, recv_sem):
        return pltpu.make_async_remote_copy(
            src_ref=ref, dst_ref=ref, send_sem=send_sem, recv_sem=recv_sem, device_id=twin,
            device_id_type=MESH)

    heads = bulk(head.at[pl.ds(0, 112), :], hs.at[0], hr.at[0])

    side = pl.ds(pl.multiple_of((p // NCOL) * HEAD, HEAD), HEAD)

    def scatter_send(half):
        return pltpu.make_async_remote_copy(
            src_ref=own.at[pl.ds(half * 8, 8), pl.ds(0, HEAD)], dst_ref=b8.at[:, side],
            send_sem=ts.at[half], recv_sem=tr.at[p // NCOL],
            device_id=(block + half, p % NCOL), device_id_type=MESH)

    def scatter_recv(h):
        lanes = b8.at[:, pl.ds(h * HEAD, HEAD)]
        return pltpu.make_async_remote_copy(
            src_ref=lanes, dst_ref=lanes, send_sem=ts.at[0], recv_sem=tr.at[h],
            device_id=(block, p % NCOL), device_id_type=MESH)

    for half in range(2):
        @pl.when(jnp.logical_not(to_self(half)))
        def _():
            scatter_send(half).start()

        @pl.when(to_self(half))
        def _():
            b8[:, side] = own[half * 8:half * 8 + 8, 0:HEAD]

    rest_in.wait()

    @pl.loop(1, 16)
    def _(b):
        lanes = pl.ds(pl.multiple_of(b * 128, 128), 128)
        own[:, lanes] = xv[pl.ds(b * 256, 128, stride=2), :].T[0:16, :]

    def piece(dist, half, which):
        rows = which * 128 + ((z + 8 - dist) % 8) * 16
        start, size = HALF[half]
        return g_ref.at[pl.ds(pl.multiple_of(rows, 16), 16), pl.ds(start, size)]

    def source(dist, half):
        start, size = HALF[half]
        return own.at[:, pl.ds(start, size)] if dist == 0 else piece(dist, half, core)

    def ring_send(direction, step, half):
        dist = step - 1 if direction == 0 else (9 - step) % 8
        slot = step if direction == 0 else 8 - step
        to = (z + 1) % 8 if direction == 0 else (z + 7) % 8
        return pltpu.make_async_remote_copy(
            src_ref=source(dist, half), dst_ref=piece(dist, half, core),
            send_sem=rs.at[direction, half, step], recv_sem=rr.at[half, slot],
            device_id=(p, to * 2 + core), device_id_type=MESH)

    def ring_recv(direction, step, half):
        slot = step if direction == 0 else 8 - step
        return pltpu.make_async_remote_copy(
            src_ref=piece(slot, half, core), dst_ref=piece(slot, half, core),
            send_sem=rs.at[direction, half, step], recv_sem=rr.at[half, slot],
            device_id=twin, device_id_type=MESH)

    def twin_send(slot, half):
        return pltpu.make_async_remote_copy(
            src_ref=source(slot, half), dst_ref=piece(slot, half, core),
            send_sem=bs.at[half, slot], recv_sem=br.at[half, slot],
            device_id=twin, device_id_type=MESH)

    def twin_recv(slot, half):
        return pltpu.make_async_remote_copy(
            src_ref=piece(slot, half, 1 - core), dst_ref=piece(slot, half, 1 - core),
            send_sem=bs.at[half, slot], recv_sem=br.at[half, slot],
            device_id=twin, device_id_type=MESH)

    def ring_step(step):
        for half in range(2):
            for direction in range(2):
                last = REACH[direction, half]
                if step <= last:
                    ring_recv(direction, step, half).wait_recv()
                    if step < last:
                        ring_send(direction, step + 1, half).start()
                    twin_send(step if direction == 0 else 8 - step, half).start()

    for half in range(2):
        ring_send(0, 1, half).start()
        ring_send(1, 1, half).start()

    heads.wait_recv()

    g8[...] = head[...].T[0:8, :]
    mine = pl.ds(pl.multiple_of(p * 8, 8), 8)
    abuf[core, mine, :] = g8[...]

    for (i, _), peer in zip(steps, row_peers):
        pltpu.make_async_remote_copy(
            src_ref=g8, dst_ref=abuf.at[core, mine, :], send_sem=as_.at[0],
            recv_sem=ar.at[i], device_id=peer, device_id_type=MESH).start()

    ring_step(1)
    for h in range(2):
        @pl.when(jnp.logical_not(from_self(h)))
        def _():
            scatter_recv(h).wait_recv()
    bbuf[mine, :] = b8[...]

    def lead(which):
        return g_ref.at[pl.ds(pl.multiple_of(which * 128, 128), 128), pl.ds(0, HEAD)]

    lead_here = pltpu.make_async_copy(head, lead(core), osem.at[0])
    lead_here.start()
    own_rows = pl.ds(pl.multiple_of(core * 128 + z * 16, 16), 16)
    own_here = pltpu.make_async_copy(
        own.at[:, pl.ds(HEAD, ROWS - HEAD)], g_ref.at[own_rows, pl.ds(HEAD, ROWS - HEAD)],
        osem.at[1])
    own_here.start()

    def lead_there(which):
        return pltpu.make_async_remote_copy(
            src_ref=head, dst_ref=lead(which), send_sem=us.at[0], recv_sem=ur.at[0],
            device_id=twin, device_id_type=MESH)

    lead_there(core).start()
    for half in range(2):
        twin_send(0, half).start()


    def a_swap(group, which):
        rows = pl.ds(pl.multiple_of(((p // 8 + 4 - group) % 4) * 64, 64), 64)
        return pltpu.make_async_remote_copy(
            src_ref=abuf.at[which, rows, :], dst_ref=abuf.at[which, rows, :],
            send_sem=us.at[1 + group], recv_sem=ur.at[1 + group], device_id=twin,
            device_id_type=MESH)

    for group in FIRST_ORDER:
        count = 56 if group == 0 else 64
        bulk(abuf.at[core, pl.ds(0, count), :], as_.at[0], ar.at[group]).wait_recv()
        a_swap(group, core).start()
    ring_step(2)

    for peer in row_peers:
        pltpu.make_async_remote_copy(
            src_ref=b8, dst_ref=bbuf.at[mine, :], send_sem=ks.at[0], recv_sem=kr.at[0],
            device_id=peer, device_id_type=MESH).start()
    b_all = bulk(bbuf.at[pl.ds(0, 248), :], ks.at[0], kr.at[0])

    for group in range(4):
        a_swap(group, 1 - core).wait_recv()

    row = lax.broadcasted_iota(jnp.int32, (256, 256), 0)
    col = lax.broadcasted_iota(jnp.int32, (256, 256), 1)
    col_order = one_hot(col == (row % 16) * NCOL + ((row // 16) % 8) * 2 + row // 128)
    rows = jnp.concatenate([
        jnp.concatenate([abuf[c, pl.ds(k, NROW, stride=8), :] for k in range(8)], 0)
        for c in range(2)], 1)
    sym[...] = jnp.where(
        row >= col, pick_right(rows, col_order), pick_left(col_order, rows, 0, 1))
    work[...] = sym[0:128, 0:128]
    late_order[...] = col_order[:, 128:256].astype(jnp.float32).T

    below[...] = jnp.zeros((128, 128), jnp.float32)
    first[...] = jnp.zeros((128, 128), jnp.float32)

    @pl.loop(0, 2)
    def _(i):
        top = pick_right(first[...], col_order[:, 0:128], 1, 1)
        inverse[0:128, :] = top
        right[...] = late_order[...] - mm(below[...], top)

        def forward(j):
            @pl.when((i == 0) & (j == SPOT[0]))
            def _():
                ring_step(3)

            @pl.when((i == 1) & (j == SPOT[1]))
            def _():
                ring_step(4)

        blocks = invert_factor([work[8 * k:8 * k + 8, :] for k in range(16)], forward)
        for k, v in enumerate(blocks):
            zd[8 * k:8 * k + 8, :] = v

        @pl.when(i == 0)
        def _():
            low = mm(sym[128:256, 0:128], zd[...], 1, 1)
            work[...] = sym[128:256, 128:256] - mm(low, low, 1, 1)
            below[...] = low
            first[...] = zd[...]

    b_all.wait_recv()

    inverse[128:256, :] = mm(zd[...], right[...])
    cols = pick_right(bbuf[...], one_hot(col == (row % 128) * 2 + row // 128))
    whole = pair(inverse[...])
    own_cols = jnp.where(row == col * NCOL + q, 1.0, 0.0)
    t = jnp.where(col < 16, own_cols, dot3(whole, pair(cols)))
    w_ref[...] = dot3(whole, pair(t), 0, 0)
    pick = one_hot(row[0:8] * NROW + p == col[0:8])
    h_ref[...] = pick_right(pick_left(pick, sym[...]), col_order, 1, 1)

    lead_there(1 - core).wait_recv()
    for half in range(2):
        for slot in range(8):
            twin_recv(slot, half).wait_recv()

    heads.wait_send()

    bulk(abuf.at[core, pl.ds(0, 248), :], as_.at[0], ar.at[0]).wait_send()
    b_all.wait_send()

    for half in range(2):
        @pl.when(jnp.logical_not(to_self(half)))
        def _():
            scatter_send(half).wait_send()

    for half in range(2):
        for direction in range(2):
            for step in range(1, REACH[direction, half] + 1):
                ring_send(direction, step, half).wait_send()
        for slot in range(8):
            twin_send(slot, half).wait_send()
    lead_there(core).wait_send()
    for group in range(4):
        a_swap(group, core).wait_send()
    lead_here.wait()
    own_here.wait()


def panel(x):
    dma = pltpu.SemaphoreType.DMA
    f32 = jnp.float32
    return pl.pallas_call(
        panel_kernel,
        out_shape=(
            jax.ShapeDtypeStruct((256, ROWS), f32),
            jax.ShapeDtypeStruct((256, 256), f32),
            jax.ShapeDtypeStruct((8, 256), f32),
        ),
        in_specs=[pl.BlockSpec(memory_space=pltpu.HBM)],
        out_specs=(
            pl.BlockSpec(memory_space=pltpu.HBM),
            pl.BlockSpec(memory_space=pltpu.VMEM),
            pl.BlockSpec(memory_space=pltpu.VMEM),
        ),
        scratch_shapes=[
            pltpu.VMEM((2 * ROWS, 128), f32),
            pltpu.VMEM((16, ROWS), f32),
            pltpu.VMEM((128, HEAD), f32),
            pltpu.VMEM((8, 128), f32),
            pltpu.VMEM((8, 256), f32),
            pltpu.VMEM((2, 256, 128), f32),
            pltpu.VMEM((256, 256), f32),
            pltpu.VMEM((256, 256), f32),
            pltpu.VMEM((128, 128), f32),
            pltpu.VMEM((128, 256), f32),
            pltpu.VMEM((128, 128), f32),
            pltpu.VMEM((256, 256), f32),
            pltpu.VMEM((128, 128), f32),
            pltpu.VMEM((128, 128), f32),
            pltpu.VMEM((128, 256), f32),
            dma((2,)), dma((2,)),
            dma((1,)), dma((1,)),
            dma((2, 2, 5)), dma((2, 8)),
            dma((2, 8)), dma((2, 8)),
            dma((1,)), dma((4,)),
            dma((1,)), dma((1,)),
            dma((2,)), dma((2,)),
            dma((5,)), dma((5,)),
        ],
        compiler_params=pltpu.CompilerParams(
            collective_id=0, has_side_effects=True, vmem_limit_bytes=24 << 20),
        name="panel",
    )(pltpu.with_memory_space_constraint(x, pltpu.HBM))


def pair(v):
    high = v.astype(jnp.bfloat16)
    return high, (v - high.astype(jnp.float32)).astype(jnp.bfloat16)


def dot3(a, b, ca=1, cb=0):
    def one(u, v):
        return lax.dot_general(
            u, v, (((ca,), (cb,)), ((), ())), preferred_element_type=jnp.float32)

    return one(a[0], b[0]) + (one(a[0], b[1]) + one(a[1], b[0]))


def update_kernel(g_ref, w_ref, h_ref, x_ref, o_ref, ov, sem):
    p = lax.axis_index("row")
    q = lax.axis_index("col")
    size = STRIP
    weights = pair(w_ref[...])
    copies = []
    for t in range(ROWS // size):
        acc = dot3(pair(g_ref[:, t * size:(t + 1) * size]), weights, 0, 0)
        start = 2 * t * size
        row = (t * size + lax.broadcasted_iota(jnp.int32, (size, 128), 0)) * NROW + p
        lane = lax.broadcasted_iota(jnp.int32, (size, 128), 1)
        left = jnp.where(
            lane < 16, acc[:, :128], x_ref[pl.ds(start, size, stride=2), :] - acc[:, :128])
        right = x_ref[pl.ds(start + 1, size, stride=2), :] - acc[:, 128:]
        if t * size * NROW < COLS * NCOL:
            left = jnp.where(row >= lane * NCOL + q, left, 0.0)
            right = jnp.where(row >= (lane + 128) * NCOL + q, right, 0.0)
        ov[pl.ds(start, size, stride=2), :] = left
        ov[pl.ds(start + 1, size, stride=2), :] = right
        if t == 0:
            keep = (row[0:8] >= lane[0:8] * NCOL + q) & (lane[0:8] < 16)
            ov[pl.ds(0, 8, stride=2), :] = jnp.where(
                keep, mm(h_ref[...], w_ref[:, 0:128]), 0.0)
        copies.append(pltpu.make_async_copy(
            ov.at[pl.ds(start, 2 * size)], o_ref.at[pl.ds(start, 2 * size)], sem.at[t]))
        copies[-1].start()
    for copy in copies:
        copy.wait()


def update(g, w, h, x):
    vmem = pl.BlockSpec(memory_space=pltpu.VMEM)
    return pl.pallas_call(
        update_kernel,
        out_shape=jax.ShapeDtypeStruct((2 * ROWS, 128), jnp.float32),
        in_specs=[vmem, vmem, vmem, vmem],
        out_specs=pl.BlockSpec(memory_space=pltpu.HBM),
        scratch_shapes=[
            pltpu.VMEM((2 * ROWS, 128), jnp.float32), pltpu.SemaphoreType.DMA((ROWS // STRIP,))],
        compiler_params=pltpu.CompilerParams(vmem_limit_bytes=24 << 20),
        name="update",
    )(g, w, h, x)


def body(window):
    x = window.reshape(2 * ROWS, 128)
    g, w, h = panel(x)
    return update(g, w, h, x).reshape(1, ROWS, 1, COLS)


def solution(mesh):
    spec = P("row", None, "col", None)
    return jax.shard_map(body, mesh=mesh, in_specs=(spec,), out_specs=spec, check_vma=False)
```

```python
import jax
import jax.numpy as jnp
from jax import lax
from jax.experimental import pallas as pl
from jax.experimental.pallas import tpu as pltpu
from jax.sharding import PartitionSpec as P

MESH = pl.DeviceIdType.MESH
NROW = 32
NCOL = 16
ROWS = 2048
COLS = 256
HEAD = 128
STRIP = 256
HALF = ((128, 1024), (1152, 896))
FIRST_ORDER = (2, 1, 3, 0)
SECOND_ORDER = (4, 3, 5, 2, 6, 1, 7, 0)
REACH = {(0, 0): 4, (1, 0): 3, (0, 1): 3, (1, 1): 4}
SPOT = (11, 10)
HIGH = lax.Precision.HIGHEST


def mm(a, b, ca=1, cb=0):
    return lax.dot_general(a, b, (((ca,), (cb,)), ((), ())), precision=HIGH, preferred_element_type=jnp.float32)

def lane_bcast(v, c):
    return jnp.broadcast_to(v[:, c:c+1], (8, 128))

def sub_bcast(v, r):
    return jnp.broadcast_to(v[r:r+1, :], (8, 128))

def invert_factor(m, forward):
    lane = lax.broadcasted_iota(jnp.int32, (8, 128), 1)
    sub = lax.broadcasted_iota(jnp.int32, (8, 128), 0)
    m = list(m)
    out = []
    for j in range(16):
        if j in SPOT:
            forward(j)
        inside = (lane >= 8*j) & (lane < 8*j+8)
        own = [lane_bcast(m[j], 8*j+k) for k in range(8)]
        e = {(i, k): sub_bcast(own[k], i) for k in range(8) for i in range(k, 8)}
        r = []
        for k in range(8):
            rk = lax.rsqrt(e[k, k])
            r.append(rk)
            for i in range(k+1, 8):
                e[i, k] = e[i, k] * rk
            for c in range(k+1, 8):
                for i in range(c, 8):
                    e[i, c] = e[i, c] - e[i, k] * e[c, k]
        row = jnp.where(inside, jnp.where(lane == sub + 8*j, 1.0, 0.0), m[j])
        final = jnp.zeros((8, 128), jnp.float32)
        ups = []
        for k in range(8):
            u = sub_bcast(row, k) * r[k]
            ups.append(u)
            final = jnp.where(sub == k, u, final)
            if k < 7:
                l = own[k] * r[k]
                row = row - l * u
                for c in range(k+1, 8):
                    own[c] = own[c] - l * e[c, k]
        out.append(jnp.where(lane < 8*j+8, final, 0.0))
        for i in range(j+1, 16):
            d = [lane_bcast(m[i], 8*j+k) for k in range(8)]
            acc = jnp.where(inside, 0.0, m[i])
            for k in range(8):
                l = d[k] * r[k]
                acc = acc - l * ups[k]
                for c in range(k+1, 8):
                    d[c] = d[c] - l * e[c, k]
            m[i] = acc
    return out


def parts(v):
    high = v.astype(jnp.bfloat16)
    rest = v - high.astype(jnp.float32)
    middle = rest.astype(jnp.bfloat16)
    return high, middle, (rest - middle.astype(jnp.float32)).astype(jnp.bfloat16)


def one_hot(match):
    return jnp.where(match, 1.0, 0.0).astype(jnp.bfloat16)


def pick_left(chosen, v, ca=1, cb=0):
    return sum(
        lax.dot_general(chosen, part, (((ca,), (cb,)), ((), ())), preferred_element_type=jnp.float32)
        for part in parts(v))


def pick_right(v, chosen, ca=1, cb=0):
    return sum(
        lax.dot_general(part, chosen, (((ca,), (cb,)), ((), ())), preferred_element_type=jnp.float32)
        for part in parts(v))


def panel_kernel(
    x_ref, g_ref, w_ref, h_ref,
    xv, own, head, g8, b8, abuf, bbuf, sym, work, right, zd, inverse, below, first, late_order,
    xsem, osem, hs, hr, rs, rr, bs, br, as_, ar, ks, kr, ts, tr, us, ur,
):
    p = lax.axis_index("row")
    q = lax.axis_index("col")
    z = q // 2
    core = q % 2
    twin = (p, z * 2 + 1 - core)
    block = core * 16 + z * 2
    feeder = 2 * ((p % NCOL) // 2) + p // NCOL

    def to_self(half):
        return (block + half == p) & (p % NCOL == q)

    def from_self(h):
        return (q + 16 * h == p) & (feeder == q)

    head_in = pltpu.make_async_copy(x_ref.at[pl.ds(0, 256)], xv.at[pl.ds(0, 256)], xsem.at[0])
    rest_in = pltpu.make_async_copy(x_ref.at[pl.ds(256, 3840)], xv.at[pl.ds(256, 3840)], xsem.at[1])
    head_in.start()
    rest_in.start()

    firsts = [lax.rem(p // 8 + i, 4) * 8 for i in range(4)]
    seconds = [lax.rem(p % 8 + j, 8) for j in range(8)]
    steps = [(i, j) for i in FIRST_ORDER for j in SECOND_ORDER if i + j > 0]
    row_peers = [(firsts[i] + seconds[j], q) for i, j in steps]
    z_peers = [(p, lax.rem(z + j, 8) * 2 + core) for j in SECOND_ORDER if j > 0]

    barrier = pltpu.get_barrier_semaphore()
    for peer in z_peers + [twin]:
        pl.semaphore_signal(barrier, inc=1, device_id=peer, device_id_type=MESH)

    waits = 7 + 1 + NROW - 1
    for half in range(2):
        @pl.when(jnp.logical_not(to_self(half)))
        def _():
            pl.semaphore_signal(
                barrier, inc=1, device_id=(block + half, p % NCOL), device_id_type=MESH)

        @pl.when(jnp.logical_not(from_self(half)))
        def _():
            pl.semaphore_signal(
                barrier, inc=1, device_id=(q + 16 * half, feeder), device_id_type=MESH)

        waits += jnp.where(to_self(half), 0, 1) + jnp.where(from_self(half), 0, 1)

    for peer in row_peers:
        pl.semaphore_signal(barrier, inc=1, device_id=peer, device_id_type=MESH)

    head_in.wait()
    own[:, 0:HEAD] = xv[pl.ds(0, HEAD, stride=2), :].T[0:16, :]
    head[pl.ds(pl.multiple_of(z * 16, 16), 16), :] = own[:, 0:HEAD]
    pl.semaphore_wait(barrier, waits)

    z_rows = pl.ds(pl.multiple_of(z * 16, 16), 16)
    head_sends = [
        pltpu.make_async_remote_copy(
            src_ref=own.at[:, pl.ds(0, HEAD)], dst_ref=head.at[z_rows, :], send_sem=hs.at[0],
            recv_sem=hr.at[0], device_id=peer, device_id_type=MESH)
        for peer in z_peers]
    for copy in head_sends:
        copy.start()

    def bulk(ref, send_sem, recv_sem):
        return pltpu.make_async_remote_copy(
            src_ref=ref, dst_ref=ref, send_sem=send_sem, recv_sem=recv_sem, device_id=twin,
            device_id_type=MESH)

    heads = bulk(head.at[pl.ds(0, 112), :], hs.at[0], hr.at[0])

    side = pl.ds(pl.multiple_of((p // NCOL) * HEAD, HEAD), HEAD)

    def scatter_send(half):
        return pltpu.make_async_remote_copy(
            src_ref=own.at[pl.ds(half * 8, 8), pl.ds(0, HEAD)], dst_ref=b8.at[:, side],
            send_sem=ts.at[half], recv_sem=tr.at[p // NCOL],
            device_id=(block + half, p % NCOL), device_id_type=MESH)

    def scatter_recv(h):
        lanes = b8.at[:, pl.ds(h * HEAD, HEAD)]
        return pltpu.make_async_remote_copy(
            src_ref=lanes, dst_ref=lanes, send_sem=ts.at[0], recv_sem=tr.at[h],
            device_id=(block, p % NCOL), device_id_type=MESH)

    for half in range(2):
        @pl.when(jnp.logical_not(to_self(half)))
        def _():
            scatter_send(half).start()

        @pl.when(to_self(half))
        def _():
            b8[:, side] = own[half * 8:half * 8 + 8, 0:HEAD]

    rest_in.wait()

    @pl.loop(1, 16)
    def _(b):
        lanes = pl.ds(pl.multiple_of(b * 128, 128), 128)
        own[:, lanes] = xv[pl.ds(b * 256, 128, stride=2), :].T[0:16, :]

    def piece(dist, half, which):
        rows = which * 128 + ((z + 8 - dist) % 8) * 16
        start, size = HALF[half]
        return g_ref.at[pl.ds(pl.multiple_of(rows, 16), 16), pl.ds(start, size)]

    def source(dist, half):
        start, size = HALF[half]
        return own.at[:, pl.ds(start, size)] if dist == 0 else piece(dist, half, core)

    def ring_send(direction, step, half):
        dist = step - 1 if direction == 0 else (9 - step) % 8
        slot = step if direction == 0 else 8 - step
        to = (z + 1) % 8 if direction == 0 else (z + 7) % 8
        return pltpu.make_async_remote_copy(
            src_ref=source(dist, half), dst_ref=piece(dist, half, core),
            send_sem=rs.at[direction, half, step], recv_sem=rr.at[half, slot],
            device_id=(p, to * 2 + core), device_id_type=MESH)

    def ring_recv(direction, step, half):
        slot = step if direction == 0 else 8 - step
        return pltpu.make_async_remote_copy(
            src_ref=piece(slot, half, core), dst_ref=piece(slot, half, core),
            send_sem=rs.at[direction, half, step], recv_sem=rr.at[half, slot],
            device_id=twin, device_id_type=MESH)

    def twin_send(slot, half):
        return pltpu.make_async_remote_copy(
            src_ref=source(slot, half), dst_ref=piece(slot, half, core),
            send_sem=bs.at[half, slot], recv_sem=br.at[half, slot],
            device_id=twin, device_id_type=MESH)

    def twin_recv(slot, half):
        return pltpu.make_async_remote_copy(
            src_ref=piece(slot, half, 1 - core), dst_ref=piece(slot, half, 1 - core),
            send_sem=bs.at[half, slot], recv_sem=br.at[half, slot],
            device_id=twin, device_id_type=MESH)

    def ring_step(step):
        for half in range(2):
            for direction in range(2):
                last = REACH[direction, half]
                if step <= last:
                    ring_recv(direction, step, half).wait_recv()
                    if step < last:
                        ring_send(direction, step + 1, half).start()
                    twin_send(step if direction == 0 else 8 - step, half).start()

    for half in range(2):
        ring_send(0, 1, half).start()
        ring_send(1, 1, half).start()

    heads.wait_recv()

    g8[...] = head[...].T[0:8, :]
    mine = pl.ds(pl.multiple_of(p * 8, 8), 8)
    abuf[core, mine, :] = g8[...]

    for (i, _), peer in zip(steps, row_peers):
        pltpu.make_async_remote_copy(
            src_ref=g8, dst_ref=abuf.at[core, mine, :], send_sem=as_.at[0],
            recv_sem=ar.at[i], device_id=peer, device_id_type=MESH).start()

    ring_step(1)
    for h in range(2):
        @pl.when(jnp.logical_not(from_self(h)))
        def _():
            scatter_recv(h).wait_recv()
    bbuf[mine, :] = b8[...]

    def lead(which):
        return g_ref.at[pl.ds(pl.multiple_of(which * 128, 128), 128), pl.ds(0, HEAD)]

    lead_here = pltpu.make_async_copy(head, lead(core), osem.at[0])
    lead_here.start()
    own_rows = pl.ds(pl.multiple_of(core * 128 + z * 16, 16), 16)
    own_here = pltpu.make_async_copy(
        own.at[:, pl.ds(HEAD, ROWS - HEAD)], g_ref.at[own_rows, pl.ds(HEAD, ROWS - HEAD)],
        osem.at[1])
    own_here.start()

    def lead_there(which):
        return pltpu.make_async_remote_copy(
            src_ref=head, dst_ref=lead(which), send_sem=us.at[0], recv_sem=ur.at[0],
            device_id=twin, device_id_type=MESH)

    lead_there(core).start()
    for half in range(2):
        twin_send(0, half).start()


    def a_swap(group, which):
        rows = pl.ds(pl.multiple_of(((p // 8 + 4 - group) % 4) * 64, 64), 64)
        return pltpu.make_async_remote_copy(
            src_ref=abuf.at[which, rows, :], dst_ref=abuf.at[which, rows, :],
            send_sem=us.at[1 + group], recv_sem=ur.at[1 + group], device_id=twin,
            device_id_type=MESH)

    for group in FIRST_ORDER:
        count = 56 if group == 0 else 64
        bulk(abuf.at[core, pl.ds(0, count), :], as_.at[0], ar.at[group]).wait_recv()
        a_swap(group, core).start()
    ring_step(2)

    for peer in row_peers:
        pltpu.make_async_remote_copy(
            src_ref=b8, dst_ref=bbuf.at[mine, :], send_sem=ks.at[0], recv_sem=kr.at[0],
            device_id=peer, device_id_type=MESH).start()
    b_all = bulk(bbuf.at[pl.ds(0, 248), :], ks.at[0], kr.at[0])

    for group in range(4):
        a_swap(group, 1 - core).wait_recv()

    row = lax.broadcasted_iota(jnp.int32, (256, 256), 0)
    col = lax.broadcasted_iota(jnp.int32, (256, 256), 1)
    col_order = one_hot(col == (row % 16) * NCOL + ((row // 16) % 8) * 2 + row // 128)
    rows = jnp.concatenate([
        jnp.concatenate([abuf[c, pl.ds(k, NROW, stride=8), :] for k in range(8)], 0)
        for c in range(2)], 1)
    sym[...] = jnp.where(
        row >= col, pick_right(rows, col_order), pick_left(col_order, rows, 0, 1))
    work[...] = sym[0:128, 0:128]
    late_order[...] = col_order[:, 128:256].astype(jnp.float32).T

    below[...] = jnp.zeros((128, 128), jnp.float32)
    first[...] = jnp.zeros((128, 128), jnp.float32)

    @pl.loop(0, 2)
    def _(i):
        top = pick_right(first[...], col_order[:, 0:128], 1, 1)
        inverse[0:128, :] = top
        right[...] = late_order[...] - mm(below[...], top)

        def forward(j):
            @pl.when((i == 0) & (j == SPOT[0]))
            def _():
                ring_step(3)

            @pl.when((i == 1) & (j == SPOT[1]))
            def _():
                ring_step(4)

        blocks = invert_factor([work[8 * k:8 * k + 8, :] for k in range(16)], forward)
        for k, v in enumerate(blocks):
            zd[8 * k:8 * k + 8, :] = v

        @pl.when(i == 0)
        def _():
            low = mm(sym[128:256, 0:128], zd[...], 1, 1)
            work[...] = sym[128:256, 128:256] - mm(low, low, 1, 1)
            below[...] = low
            first[...] = zd[...]

    b_all.wait_recv()

    inverse[128:256, :] = mm(zd[...], right[...])
    cols = pick_right(bbuf[...], one_hot(col == (row % 128) * 2 + row // 128))
    whole = pair(inverse[...])
    own_cols = jnp.where(row == col * NCOL + q, 1.0, 0.0)
    t = jnp.where(col < 16, own_cols, dot3(whole, pair(cols)))
    w_ref[...] = dot3(whole, pair(t), 0, 0)
    pick = one_hot(row[0:8] * NROW + p == col[0:8])
    h_ref[...] = pick_right(pick_left(pick, sym[...]), col_order, 1, 1)

    lead_there(1 - core).wait_recv()
    for half in range(2):
        for slot in range(8):
            twin_recv(slot, half).wait_recv()

    heads.wait_send()

    bulk(abuf.at[core, pl.ds(0, 248), :], as_.at[0], ar.at[0]).wait_send()
    b_all.wait_send()

    for half in range(2):
        @pl.when(jnp.logical_not(to_self(half)))
        def _():
            scatter_send(half).wait_send()

    for half in range(2):
        for direction in range(2):
            for step in range(1, REACH[direction, half] + 1):
                ring_send(direction, step, half).wait_send()
        for slot in range(8):
            twin_send(slot, half).wait_send()
    lead_there(core).wait_send()
    for group in range(4):
        a_swap(group, core).wait_send()
    lead_here.wait()
    own_here.wait()


def panel(x):
    dma = pltpu.SemaphoreType.DMA
    f32 = jnp.float32
    return pl.pallas_call(
        panel_kernel,
        out_shape=(
            jax.ShapeDtypeStruct((256, ROWS), f32),
            jax.ShapeDtypeStruct((256, 256), f32),
            jax.ShapeDtypeStruct((8, 256), f32),
        ),
        in_specs=[pl.BlockSpec(memory_space=pltpu.HBM)],
        out_specs=(
            pl.BlockSpec(memory_space=pltpu.HBM),
            pl.BlockSpec(memory_space=pltpu.VMEM),
            pl.BlockSpec(memory_space=pltpu.VMEM),
        ),
        scratch_shapes=[
            pltpu.VMEM((2 * ROWS, 128), f32),
            pltpu.VMEM((16, ROWS), f32),
            pltpu.VMEM((128, HEAD), f32),
            pltpu.VMEM((8, 128), f32),
            pltpu.VMEM((8, 256), f32),
            pltpu.VMEM((2, 256, 128), f32),
            pltpu.VMEM((256, 256), f32),
            pltpu.VMEM((256, 256), f32),
            pltpu.VMEM((128, 128), f32),
            pltpu.VMEM((128, 256), f32),
            pltpu.VMEM((128, 128), f32),
            pltpu.VMEM((256, 256), f32),
            pltpu.VMEM((128, 128), f32),
            pltpu.VMEM((128, 128), f32),
            pltpu.VMEM((128, 256), f32),
            dma((2,)), dma((2,)),
            dma((1,)), dma((1,)),
            dma((2, 2, 5)), dma((2, 8)),
            dma((2, 8)), dma((2, 8)),
            dma((1,)), dma((4,)),
            dma((1,)), dma((1,)),
            dma((2,)), dma((2,)),
            dma((5,)), dma((5,)),
        ],
        compiler_params=pltpu.CompilerParams(
            collective_id=0, has_side_effects=True, vmem_limit_bytes=24 << 20),
        name="panel",
    )(pltpu.with_memory_space_constraint(x, pltpu.HBM))


def pair(v):
    high = v.astype(jnp.bfloat16)
    return high, (v - high.astype(jnp.float32)).astype(jnp.bfloat16)


def dot3(a, b, ca=1, cb=0):
    def one(u, v):
        return lax.dot_general(
            u, v, (((ca,), (cb,)), ((), ())), preferred_element_type=jnp.float32)

    return one(a[0], b[0]) + (one(a[0], b[1]) + one(a[1], b[0]))


def update_kernel(g_ref, w_ref, h_ref, x_ref, o_ref, ov, sem):
    p = lax.axis_index("row")
    q = lax.axis_index("col")
    size = STRIP
    weights = pair(w_ref[...])
    copies = []
    for t in range(ROWS // size):
        acc = dot3(pair(g_ref[:, t * size:(t + 1) * size]), weights, 0, 0)
        start = 2 * t * size
        row = (t * size + lax.broadcasted_iota(jnp.int32, (size, 128), 0)) * NROW + p
        lane = lax.broadcasted_iota(jnp.int32, (size, 128), 1)
        left = jnp.where(
            lane < 16, acc[:, :128], x_ref[pl.ds(start, size, stride=2), :] - acc[:, :128])
        right = x_ref[pl.ds(start + 1, size, stride=2), :] - acc[:, 128:]
        if t * size * NROW < COLS * NCOL:
            left = jnp.where(row >= lane * NCOL + q, left, 0.0)
            right = jnp.where(row >= (lane + 128) * NCOL + q, right, 0.0)
        ov[pl.ds(start, size, stride=2), :] = left
        ov[pl.ds(start + 1, size, stride=2), :] = right
        if t == 0:
            keep = (row[0:8] >= lane[0:8] * NCOL + q) & (lane[0:8] < 16)
            ov[pl.ds(0, 8, stride=2), :] = jnp.where(
                keep, mm(h_ref[...], w_ref[:, 0:128]), 0.0)
        copies.append(pltpu.make_async_copy(
            ov.at[pl.ds(start, 2 * size)], o_ref.at[pl.ds(start, 2 * size)], sem.at[t]))
        copies[-1].start()
    for copy in copies:
        copy.wait()


def update(g, w, h, x):
    vmem = pl.BlockSpec(memory_space=pltpu.VMEM)
    return pl.pallas_call(
        update_kernel,
        out_shape=jax.ShapeDtypeStruct((2 * ROWS, 128), jnp.float32),
        in_specs=[vmem, vmem, vmem, vmem],
        out_specs=pl.BlockSpec(memory_space=pltpu.HBM),
        scratch_shapes=[
            pltpu.VMEM((2 * ROWS, 128), jnp.float32), pltpu.SemaphoreType.DMA((ROWS // STRIP,))],
        compiler_params=pltpu.CompilerParams(vmem_limit_bytes=24 << 20),
        name="update",
    )(g, w, h, x)


def body(window):
    x = window.reshape(2 * ROWS, 128)
    g, w, h = panel(x)
    return update(g, w, h, x).reshape(1, ROWS, 1, COLS)


def solution(mesh):
    spec = P("row", None, "col", None)
    return jax.shard_map(body, mesh=mesh, in_specs=(spec,), out_specs=spec, check_vma=False)
```
